32 devices in a mesh: bank: 8 (over z, y), feat: 4 (over x, core).
Axes of the slice: x: 2, y: 2, z: 4, core: 2. Of those that a mesh axis runs over, the one named last changes fastest.
Arguments:
- bank_rows: bfloat16 [12288, 1536], P('bank', 'feat'), may hold values from -16 to 16
- offsets: int32 [17], replicated, may hold values from 0 to 24576, as said below
Outputs:
- whitened: bfloat16 [12288, 1536], P('bank', 'feat')
The draws below stay inside these ranges and needn't reach their ends.
Inputs may be any that keep to these rules, and one draw needn't show every extreme that they name: offsets[0] = 0 and offsets[16] = 24576; cluster k holds the rows offsets[k] to offsets[k+1] - 1, and every cluster holds 1152 to 1920 rows, both counts reached in every draw.
All inputs are finite; a program needn't handle non-finite values.
Results may differ from the reference program's by a relative error of at most 0.0058.
Values may be sent and summed in bfloat16 or wider, within the bound.
A program may use at most 128 MiB of HBM per device.

```python
import jax
import jax.numpy as jnp
from jax import lax

D = 768
ROWS_DEV = 3072
ROWS = 24576
CLUSTERS = 16


def draw_offsets(key, part):
    size_key, order_key = jax.random.split(key)
    half_rows = ROWS_DEV // 2
    spread_rows = ROWS_DEV // 8
    deviation = jax.random.randint(size_key, (CLUSTERS // 2,), 0, spread_rows + 1, dtype=jnp.int32)
    deviation = deviation.at[0].set(spread_rows)
    row_counts = jnp.stack([half_rows + deviation, half_rows - deviation], axis=1).reshape(-1)
    shuffle = jax.random.permutation(order_key, CLUSTERS)
    row_counts = row_counts[shuffle]
    return jnp.concatenate([jnp.zeros((1,), jnp.int32), jnp.cumsum(row_counts).astype(jnp.int32)])


def draw_bank_rows(key, part):
    noise_key, scale_key = jax.random.split(key)
    noise_values = jnp.clip(jax.random.normal(noise_key, (ROWS, D), jnp.float32), -5.0, 5.0)
    scales = jnp.exp(jax.random.uniform(scale_key, (1, D), jnp.float32, jnp.log(0.5), jnp.log(2.0)))
    mixed = noise_values + 0.6 * jnp.roll(noise_values, 1, axis=1)
    return (scales * mixed).astype(jnp.bfloat16).reshape(ROWS // 2, 2 * D)


def setup_inputs(seed: int = 0) -> dict:
    streams_of = jax.random.split(jax.random.key(seed), 3)
    bank_rows = draw_bank_rows(jax.random.fold_in(streams_of[2], 71), 0)
    offsets = draw_offsets(jax.random.fold_in(streams_of[2], 71), 0)
    return {"bank_rows": bank_rows, "offsets": offsets}


ridge_shift = 0.5

def transposed_product(left_rows, right_rows):
    return lax.dot_general(left_rows.astype(jnp.float32), right_rows.astype(jnp.float32), (((0,), (0,)), ((), ())), preferred_element_type=jnp.float32)

def add_slot(gram_tiles, term, slot_index):
    current = lax.dynamic_index_in_dim(gram_tiles, slot_index, 0, keepdims=False)
    return lax.dynamic_update_index_in_dim(gram_tiles, current + term, slot_index, 0)

def reference(bank_rows, offsets):
    full_width = bank_rows.shape[1] // 2
    total_rows = bank_rows.shape[0] * 2
    flat_rows = bank_rows.reshape(total_rows, full_width)
    cluster_count = offsets.shape[0] - 1
    block_rows = min(512, ROWS_DEV // 4)
    boundaries = offsets[1:-1]

    def labels_of(offset_row):
        positions = offset_row + jnp.arange(block_rows, dtype=jnp.int32)
        return jnp.sum((boundaries[None, :] <= positions[:, None]).astype(jnp.int32), axis=1)

    def split_rows(offset_row):
        block_data = lax.dynamic_slice_in_dim(flat_rows, offset_row, block_rows, 0)
        block_labels = labels_of(offset_row)
        lead_label = block_labels[0]
        later_mask = (block_labels != lead_label).astype(jnp.bfloat16)[:, None]
        later_rows = block_data * later_mask
        early_rows = block_data - later_rows
        return (block_data, early_rows, later_rows, lead_label)

    def gram_step(gram_tiles, offset_row):
        block_data, early_rows, later_rows, lead_label = split_rows(offset_row)
        gram_tiles = add_slot(gram_tiles, transposed_product(early_rows, block_data), lead_label)
        gram_tiles = add_slot(gram_tiles, transposed_product(later_rows, block_data), jnp.minimum(lead_label + 1, cluster_count - 1))
        return (gram_tiles, None)
    block_starts = jnp.arange(total_rows // block_rows, dtype=jnp.int32) * block_rows
    gram_tiles, _ = lax.scan(gram_step, jnp.zeros((cluster_count, full_width, full_width), jnp.float32), block_starts)
    row_counts = (offsets[1:] - offsets[:-1]).astype(jnp.float32)
    identity = jnp.eye(full_width, dtype=jnp.float32)
    covariance = gram_tiles / row_counts[:, None, None] + ridge_shift * identity
    factor = jnp.linalg.cholesky(covariance)
    inverse = lax.linalg.triangular_solve(factor, jnp.broadcast_to(identity, covariance.shape), left_side=True, lower=True)
    whitener = inverse.astype(jnp.bfloat16)

    def whiten_step(carry, offset_row):
        block_data, early_rows, later_rows, lead_label = split_rows(offset_row)
        first_factor = lax.dynamic_index_in_dim(whitener, lead_label, 0, keepdims=False)
        second_factor = lax.dynamic_index_in_dim(whitener, jnp.minimum(lead_label + 1, cluster_count - 1), 0, keepdims=False)
        product_rows = lax.dot_general(early_rows.astype(jnp.float32), first_factor.astype(jnp.float32), (((1,), (1,)), ((), ())), preferred_element_type=jnp.float32)
        product_rows = product_rows + lax.dot_general(later_rows.astype(jnp.float32), second_factor.astype(jnp.float32), (((1,), (1,)), ((), ())), preferred_element_type=jnp.float32)
        return (carry, product_rows.astype(jnp.bfloat16))
    _, pieces = lax.scan(whiten_step, jnp.int32(0), block_starts)
    return pieces.reshape(total_rows // 2, 2 * full_width)
```

```python
import functools

import jax
import jax.numpy as jnp
from jax import lax
from jax.experimental import pallas as pl
from jax.experimental.pallas import tpu as pltpu
from jax.sharding import PartitionSpec as P

TOUCH = 4
BLOCK = 128
SUB = 8
WINDOW = 4
ridge_shift = 0.5


MESH = pl.DeviceIdType.MESH
GATHER_CHUNKS = 6


def slot_of(offsets, role, row_start, rows_dev):
    clusters = offsets.shape[0] - 1

    def count(k, found):
        bound = offsets[k]
        first, last = found
        first = first + (bound <= row_start).astype(jnp.int32)
        last = last + (bound <= row_start + rows_dev - 1).astype(jnp.int32)
        return first, last

    first, last = lax.fori_loop(1, clusters, count, (jnp.int32(0), jnp.int32(0)))
    is_last = role == TOUCH - 1
    label = jnp.where(is_last, last, jnp.minimum(first + role, last))
    used = jnp.logical_or(is_last, first + role < last)
    low = jnp.clip(offsets[label] - row_start, 0, rows_dev)
    high = jnp.clip(offsets[label + 1] - row_start, 0, rows_dev)
    return low, jnp.where(used, high, low), label


def own_role():
    feat = lax.axis_index("feat")
    return jnp.where(lax.axis_index("bank") % 2 == 0, feat, TOUCH - 1 - feat)


def neighbours():
    bank, feat = lax.axis_index("bank"), lax.axis_index("feat")
    sibling = feat + 1 - 2 * (feat % 2)
    return bank, sibling, (feat + 2) % TOUCH, (sibling + 2) % TOUCH


def greet(bank, others):
    barrier = pltpu.get_barrier_semaphore()
    for other in others:
        pl.semaphore_signal(barrier, inc=1, device_id=(bank, other), device_id_type=MESH)
    pl.semaphore_wait(barrier, len(others))


def upper_blocks(width):
    blocks = width // BLOCK
    return [(i, k) for i in range(blocks) for k in range(i, blocks)]


def ordered(first, second, swap):
    left = jnp.where(swap, second, first)
    right = jnp.where(swap, first, second)
    return jnp.concatenate([left, right], axis=1)


def gram_kernel(
    offsets, own, packed_ref, near_ref, kept, near, across, far, gram, send, receive, local
):
    bank, sibling, partner, _ = neighbours()
    greet(bank, (sibling, partner))
    pair_rows, half = own.shape
    piece = pair_rows // GATHER_CHUNKS
    rows_dev = 2 * pair_rows

    def remote(source, target, place, device):
        return pltpu.make_async_remote_copy(
            src_ref=source,
            dst_ref=target,
            send_sem=send.at[place],
            recv_sem=receive.at[place],
            device_id=(bank, device),
            device_id_type=MESH,
        )

    def part(i):
        return pl.ds(pl.multiple_of(i * piece, piece), piece)

    def crossing(i):
        return remote(own.at[part(i), :], across.at[part(i), :], i, partner)

    def passing(i):
        return remote(across.at[part(i), :], far.at[part(i), :], GATHER_CHUNKS + i, sibling)

    beside = remote(own, near, 2 * GATHER_CHUNKS, sibling)
    fetch = pltpu.make_async_copy(own, kept, local.at[0])
    keep_near = pltpu.make_async_copy(near, near_ref, local.at[1])
    beside.start()

    @pl.loop(0, GATHER_CHUNKS)
    def _(i):
        crossing(i).start()

    fetch.start()
    low, high, _ = slot_of(offsets, own_role(), bank * rows_dev, rows_dev)
    feat = lax.axis_index("feat")
    parity = feat // 2
    gram[...] = jnp.zeros_like(gram)

    def add(first, second, i, shift):
        data = ordered(first[part(i), :], second[part(i), :], feat % 2 == 1)
        row = 2 * (i * piece + lax.broadcasted_iota(jnp.int32, (piece, 1), 0)) + shift
        inside = jnp.logical_and(row >= low, row < high)
        data = jnp.where(inside, data, jnp.zeros_like(data))
        gram[...] += lax.dot_general(
            data, data, (((0,), (0,)), ((), ())), preferred_element_type=jnp.float32
        )

    fetch.wait()
    beside.wait_recv()
    keep_near.start()

    @pl.loop(0, GATHER_CHUNKS)
    def _(i):
        add(kept, near, i, parity)

    @pl.loop(0, GATHER_CHUNKS + 1)
    def _(i):
        @pl.when(i < GATHER_CHUNKS)
        def _():
            crossing(i).wait_recv()
            passing(i).start()

        @pl.when(i > 0)
        def _():
            passing(i - 1).wait_recv()
            add(across, far, i - 1, 1 - parity)

    for place, (i, k) in enumerate(upper_blocks(2 * half)):
        packed_ref[place] = gram[i * BLOCK : (i + 1) * BLOCK, k * BLOCK : (k + 1) * BLOCK]

    @pl.loop(0, GATHER_CHUNKS)
    def _(i):
        crossing(i).wait_send()
        passing(i).wait_send()

    beside.wait_send()
    keep_near.wait()


def own_gram(offsets, own):
    width = 2 * own.shape[1]
    packed = (len(upper_blocks(width)), BLOCK, BLOCK)
    anywhere = pl.BlockSpec(memory_space=pl.ANY)
    return pl.pallas_call(
        gram_kernel,
        in_specs=[
            pl.BlockSpec(memory_space=pltpu.SMEM),
            pl.BlockSpec(memory_space=pltpu.HBM),
        ],
        out_specs=[pl.BlockSpec(memory_space=pltpu.VMEM), anywhere],
        out_shape=[
            jax.ShapeDtypeStruct(packed, jnp.float32),
            jax.ShapeDtypeStruct(own.shape, own.dtype),
        ],
        scratch_shapes=[pltpu.VMEM(own.shape, own.dtype)] * 4
        + [
            pltpu.VMEM((width, width), jnp.float32),
            pltpu.SemaphoreType.DMA((2 * GATHER_CHUNKS + 1,)),
            pltpu.SemaphoreType.DMA((2 * GATHER_CHUNKS + 1,)),
            pltpu.SemaphoreType.DMA((2,)),
        ],
        compiler_params=pltpu.CompilerParams(
            collective_id=0, has_side_effects=True, vmem_limit_bytes=32 << 20
        ),
    )(offsets, own)


def split_rows(value):
    high = value.astype(jnp.bfloat16).astype(jnp.float32)
    rest = value - high
    middle = rest.astype(jnp.bfloat16).astype(jnp.float32)
    low = (rest - middle).astype(jnp.bfloat16).astype(jnp.float32)
    return high, middle, low


def factor_block(work):
    panels = BLOCK // SUB
    shape = (SUB, BLOCK)
    lane = lax.broadcasted_iota(jnp.int32, shape, 1)
    sub = lax.broadcasted_iota(jnp.int32, shape, 0)

    def column(tile, c):
        return jnp.broadcast_to(tile[:, c : c + 1], shape)

    def row(tile, i):
        return jnp.broadcast_to(tile[i : i + 1, :], shape)

    tiles = [work[p * SUB : (p + 1) * SUB, :] for p in range(panels)]
    entry_columns = [column(tiles[0], k) for k in range(SUB)]
    for p in range(panels):
        base = p * SUB
        here = jnp.logical_and(lane >= base, lane < base + SUB)
        entry = {(i, k): row(entry_columns[k], i) for i in range(SUB) for k in range(i, SUB)}
        near = range(p + 1, min(p + 1 + WINDOW, panels))
        factors = {r: [column(tiles[r], base + k) for k in range(SUB)] for r in near}
        following = [column(tiles[p + 1], base + SUB + k) for k in range(SUB)] if near else []
        own = jnp.where(here, (lane - base == sub).astype(jnp.float32), tiles[p])
        lines = [row(own, k) for k in range(SUB)]
        for r in near:
            tiles[r] = jnp.where(here, 0.0, tiles[r])
        for k in range(SUB):
            inverse_root = lax.rsqrt(entry[k, k])
            coefficient = {i: entry[k, i] * inverse_root for i in range(k + 1, SUB)}
            for i in range(k + 1, SUB):
                for m in range(i, SUB):
                    entry[i, m] = entry[i, m] - coefficient[i] * coefficient[m]
            lines[k] = lines[k] * inverse_root
            for i in range(k + 1, SUB):
                lines[i] = lines[i] - coefficient[i] * lines[k]
            for r in near:
                scaled = factors[r][k] * inverse_root
                for i in range(k + 1, SUB):
                    factors[r][i] = factors[r][i] - coefficient[i] * scaled
                if r == p + 1:
                    for m in range(SUB):
                        following[m] = following[m] - scaled * row(scaled, m)
                tiles[r] = tiles[r] - scaled * lines[k]
        entry_columns = following
        done = lines[SUB - 1]
        for k in range(SUB - 1):
            done = jnp.where(sub == k, lines[k], done)
        work[base : base + SUB, :] = jnp.where(lane < base + SUB, done, 0.0)
        if p + 1 + WINDOW < panels:
            high, middle, low = split_rows(done)
            left = jnp.concatenate([high, high, middle, high, middle, low], axis=0)
            right = jnp.concatenate([high, middle, high, low, middle, high], axis=0)
            update = lax.dot_general(
                left.astype(jnp.bfloat16),
                right.astype(jnp.bfloat16),
                (((0,), (0,)), ((), ())),
                preferred_element_type=jnp.float32,
            )
            for r in range(p + 1 + WINDOW, panels):
                tiles[r] = jnp.where(here, 0.0, tiles[r]) - update[r * SUB : (r + 1) * SUB, :]


def whitener_kernel(
    rows_dev, bank_count, offsets, own_ref, rows_ref, other, matrix, work, final,
    swap_send, swap_receive, send, receive, local,
):
    width = matrix.shape[0]
    half = width // 2
    blocks = width // BLOCK
    strips = half // BLOCK
    bank, sibling, partner, diagonal = neighbours()
    feat = lax.axis_index("feat")
    role = own_role()
    meets_left = jnp.logical_and(role == 0, bank > 0)
    meets_right = jnp.logical_and(role == TOUCH - 1, bank < bank_count - 1)
    meets = jnp.logical_or(meets_left, meets_right)
    met = jnp.where(meets_left, bank - 1, bank + 1)

    barrier = pltpu.get_barrier_semaphore()
    for device in (sibling, partner, diagonal):
        pl.semaphore_signal(barrier, inc=1, device_id=(bank, device), device_id_type=MESH)

    def swap(i):
        place = sum(blocks - k for k in range(i))
        span = pl.ds(place, blocks - i)
        return pltpu.make_async_remote_copy(
            src_ref=own_ref.at[span],
            dst_ref=other.at[span],
            send_sem=swap_send.at[i],
            recv_sem=swap_receive.at[i],
            device_id=(met, feat),
            device_id_type=MESH,
        )

    @pl.when(meets)
    def _():
        pl.semaphore_signal(barrier, inc=1, device_id=(met, feat), device_id_type=MESH)
        pl.semaphore_wait(barrier, 4)
        for i in range(blocks):
            swap(i).start()

    @pl.when(jnp.logical_not(meets))
    def _():
        pl.semaphore_wait(barrier, 3)
        other[...] = jnp.zeros_like(other)

    row_start = bank * rows_dev
    _, _, label = slot_of(offsets, role, row_start, rows_dev)
    left_open = jnp.logical_and(role == 0, offsets[label] < row_start)
    right_open = jnp.logical_and(role == TOUCH - 1, offsets[label + 1] > row_start + rows_dev)
    joined = jnp.logical_or(left_open, right_open)
    count = (offsets[label + 1] - offsets[label]).astype(jnp.float32)
    eye = (
        lax.broadcasted_iota(jnp.int32, (BLOCK, BLOCK), 0)
        == lax.broadcasted_iota(jnp.int32, (BLOCK, BLOCK), 1)
    ).astype(jnp.float32)

    def strip(place, i, device):
        columns = pl.ds(0, (i + 1) * BLOCK)
        return pltpu.make_async_remote_copy(
            src_ref=final.at[pl.ds(i * BLOCK, BLOCK), columns],
            dst_ref=rows_ref.at[feat, pl.ds(i % strips * BLOCK, BLOCK), columns],
            send_sem=send.at[place, i % strips],
            recv_sem=receive.at[place, i % strips],
            device_id=(bank, device),
            device_id_type=MESH,
        )

    def stay(i):
        columns = pl.ds(0, (i + 1) * BLOCK)
        return pltpu.make_async_copy(
            final.at[pl.ds(i * BLOCK, BLOCK), columns],
            rows_ref.at[feat, pl.ds(i % strips * BLOCK, BLOCK), columns],
            local.at[i % strips],
        )

    @pl.loop(0, blocks)
    def _(j):
        here = pl.ds(pl.multiple_of(j * BLOCK, BLOCK), BLOCK)
        for i in range(blocks):

            @pl.when(j == i)
            def _():
                @pl.when(meets)
                def _():
                    swap(i).wait_recv()

                for k in range(i, blocks):
                    place = sum(blocks - n for n in range(i)) + k - i
                    total = own_ref[place] + jnp.where(joined, other[place], 0.0)
                    total = total / count
                    if i == k:
                        total = total + ridge_shift * eye
                    matrix[i * BLOCK : (i + 1) * BLOCK, k * BLOCK : (k + 1) * BLOCK] = total

        @pl.loop(0, j)
        def _(k):
            above = pl.ds(pl.multiple_of(k * BLOCK, BLOCK), BLOCK)
            update = lax.dot_general(
                matrix[above, here],
                matrix[above, :],
                (((0,), (0,)), ((), ())),
                precision=lax.Precision.HIGHEST,
                preferred_element_type=jnp.float32,
            )
            matrix[here, above] = jnp.zeros_like(eye)
            matrix[here, :] = matrix[here, :] - update

        work[...] = matrix[here, here]
        factor_block(work)
        matrix[here, here] = eye
        panel = lax.dot_general(
            work[...],
            matrix[here, :],
            (((1,), (0,)), ((), ())),
            precision=lax.Precision.HIGHEST,
            preferred_element_type=jnp.float32,
        )
        matrix[here, :] = panel
        final[here, :] = panel.astype(jnp.bfloat16)
        for i in range(blocks):
            mine = 0 if i < strips else 1

            @pl.when(jnp.logical_and(j == i, feat % 2 == mine))
            def _():
                strip(0, i, partner).start()
                stay(i).start()

            @pl.when(jnp.logical_and(j == i, feat % 2 != mine))
            def _():
                strip(1, i, diagonal).start()
                strip(2, i, sibling).start()

    @pl.when(meets)
    def _():
        for i in range(blocks):
            swap(i).wait_send()

    for parity in range(2):

        @pl.when(feat % 2 == parity)
        def _():
            for i in range(strips):
                mine, others = parity * strips + i, (1 - parity) * strips + i
                strip(0, mine, partner).wait_send()
                strip(1, others, diagonal).wait_send()
                strip(2, others, sibling).wait_send()
                stay(mine).wait()
            for i in range(strips):
                mine = parity * strips + i
                strip(0, mine, partner).wait_recv()
                strip(1, mine, diagonal).wait_recv()
                strip(2, mine, sibling).wait_recv()


def whitener_rows(rows_dev, width, offsets, own):
    half, blocks = width // 2, width // BLOCK
    strips = half // BLOCK
    return pl.pallas_call(
        functools.partial(whitener_kernel, rows_dev, lax.axis_size("bank")),
        in_specs=[
            pl.BlockSpec(memory_space=pltpu.SMEM),
            pl.BlockSpec(memory_space=pltpu.VMEM),
        ],
        out_specs=pl.BlockSpec(memory_space=pl.ANY),
        out_shape=jax.ShapeDtypeStruct((TOUCH, half, width), jnp.bfloat16),
        scratch_shapes=[
            pltpu.VMEM(own.shape, jnp.float32),
            pltpu.VMEM((width, width), jnp.float32),
            pltpu.VMEM((BLOCK, BLOCK), jnp.float32),
            pltpu.VMEM((width, width), jnp.bfloat16),
            pltpu.SemaphoreType.DMA((blocks,)),
            pltpu.SemaphoreType.DMA((blocks,)),
            pltpu.SemaphoreType.DMA((3, strips)),
            pltpu.SemaphoreType.DMA((3, strips)),
            pltpu.SemaphoreType.DMA((strips,)),
        ],
        compiler_params=pltpu.CompilerParams(
            collective_id=1, has_side_effects=True, vmem_limit_bytes=32 << 20
        ),
    )(offsets, own)


def whiten_kernel(offsets, own, near, factor_ref, out_ref, factors, total, bounds):
    step = pl.program_id(0)
    block_pairs, half = own.shape
    rows_dev = pl.num_programs(0) * block_pairs * 2
    bank, feat = lax.axis_index("bank"), lax.axis_index("feat")
    start = step * block_pairs * 2

    @pl.when(step == 0)
    def _():
        shape = factor_ref.shape[1:]
        row = (feat % 2) * half + lax.broadcasted_iota(jnp.int32, shape, 0)
        inside = lax.broadcasted_iota(jnp.int32, shape, 1) <= row
        for role in range(TOUCH):
            bounds[role], bounds[TOUCH + role], _ = slot_of(
                offsets, jnp.int32(role), bank * rows_dev, rows_dev
            )
        for place in range(TOUCH):
            rows = factor_ref[place]
            factors[place] = jnp.where(inside, rows, jnp.zeros_like(rows))

    total[...] = jnp.zeros_like(total)
    for role in range(TOUCH):
        low, high = bounds[role], bounds[TOUCH + role]

        @pl.when(jnp.logical_and(start < high, start + 2 * block_pairs > low))
        def _():
            place = jnp.where(bank % 2 == 0, role, TOUCH - 1 - role)
            row = start + feat // 2 + 2 * lax.broadcasted_iota(jnp.int32, (block_pairs, 1), 0)
            data = ordered(own[...], near[...], feat % 2 == 1)
            keep = jnp.logical_and(row >= low, row < high)
            data = jnp.where(keep, data, jnp.zeros_like(data))
            total[...] += lax.dot_general(
                data, factors[place], (((1,), (1,)), ((), ())), preferred_element_type=jnp.float32
            )

    out_ref[...] = total[...].astype(jnp.bfloat16)


def whiten(offsets, own, near, factor_rows):
    pair_rows, half = own.shape
    block_pairs = min(256, pair_rows)
    block = pl.BlockSpec((block_pairs, half), lambda i: (i, 0))
    return pl.pallas_call(
        whiten_kernel,
        grid=(pair_rows // block_pairs,),
        in_specs=[
            pl.BlockSpec(memory_space=pltpu.SMEM),
            block,
            block,
            pl.BlockSpec(factor_rows.shape, lambda i: (0, 0, 0)),
        ],
        out_specs=block,
        out_shape=jax.ShapeDtypeStruct((pair_rows, half), jnp.bfloat16),
        scratch_shapes=[
            pltpu.VMEM(factor_rows.shape, jnp.bfloat16),
            pltpu.VMEM((block_pairs, half), jnp.float32),
            pltpu.SMEM((2 * TOUCH,), jnp.int32),
        ],
        compiler_params=pltpu.CompilerParams(vmem_limit_bytes=32 << 20),
    )(offsets, own, near, factor_rows)


def shards(bank_rows, offsets):
    pair_rows, out_width = bank_rows.shape
    own, near = own_gram(offsets, bank_rows)
    factor_rows = whitener_rows(pair_rows * 2, 2 * out_width, offsets, own)
    return whiten(offsets, bank_rows, near, factor_rows)


def solution(mesh):
    return jax.shard_map(
        shards,
        mesh=mesh,
        in_specs=(P("bank", "feat"), P()),
        out_specs=P("bank", "feat"),
        check_vma=False,
    )
```

```python
import functools

import jax
import jax.numpy as jnp
from jax import lax
from jax.experimental import pallas as pl
from jax.experimental.pallas import tpu as pltpu
from jax.sharding import PartitionSpec as P

TOUCH = 4
BLOCK = 128
SUB = 8
WINDOW = 4
ridge_shift = 0.5


MESH = pl.DeviceIdType.MESH
AHEAD = 2
HOLD = 4


def slot_of(offsets, role, row_start, rows_dev):
    clusters = offsets.shape[0] - 1

    def count(k, found):
        bound = offsets[k]
        first, last = found
        first = first + (bound <= row_start).astype(jnp.int32)
        last = last + (bound <= row_start + rows_dev - 1).astype(jnp.int32)
        return first, last

    first, last = lax.fori_loop(1, clusters, count, (jnp.int32(0), jnp.int32(0)))
    is_last = role == TOUCH - 1
    label = jnp.where(is_last, last, jnp.minimum(first + role, last))
    used = jnp.logical_or(is_last, first + role < last)
    low = jnp.clip(offsets[label] - row_start, 0, rows_dev)
    high = jnp.clip(offsets[label + 1] - row_start, 0, rows_dev)
    return low, jnp.where(used, high, low), label


def own_role():
    feat = lax.axis_index("feat")
    return jnp.where(lax.axis_index("bank") % 2 == 0, feat, TOUCH - 1 - feat)


def neighbours():
    bank, feat = lax.axis_index("bank"), lax.axis_index("feat")
    sibling = feat + 1 - 2 * (feat % 2)
    return bank, sibling, (feat + 2) % TOUCH, (sibling + 2) % TOUCH


def ordered(first, second, swap):
    left = jnp.where(swap, second, first)
    right = jnp.where(swap, first, second)
    return jnp.concatenate([left, right], axis=1)


def split(value):
    high = value.astype(jnp.bfloat16)
    rest = value - high.astype(jnp.float32)
    middle = rest.astype(jnp.bfloat16)
    low = (rest - middle.astype(jnp.float32)).astype(jnp.bfloat16)
    return high, middle, low


def product(left, right, right_dim):
    first = jnp.concatenate([left[n] for n in (0, 0, 1, 0, 1, 2)], axis=1)
    second = jnp.concatenate([right[n] for n in (0, 1, 0, 2, 1, 0)], axis=right_dim)
    return lax.dot_general(
        first, second, (((1,), (right_dim,)), ((), ())), preferred_element_type=jnp.float32
    )


def split_rows(value):
    high = value.astype(jnp.bfloat16).astype(jnp.float32)
    rest = value - high
    middle = rest.astype(jnp.bfloat16).astype(jnp.float32)
    low = (rest - middle).astype(jnp.bfloat16).astype(jnp.float32)
    return high, middle, low


def factor_block(work):
    panels = BLOCK // SUB
    shape = (SUB, BLOCK)
    lane = lax.broadcasted_iota(jnp.int32, shape, 1)
    sub = lax.broadcasted_iota(jnp.int32, shape, 0)

    def column(tile, c):
        return jnp.broadcast_to(tile[:, c : c + 1], shape)

    def row(tile, i):
        return jnp.broadcast_to(tile[i : i + 1, :], shape)

    tiles = [work[p * SUB : (p + 1) * SUB, :] for p in range(panels)]
    entry_columns = [column(tiles[0], k) for k in range(SUB)]
    for p in range(panels):
        base = p * SUB
        here = jnp.logical_and(lane >= base, lane < base + SUB)
        entry = {(i, k): row(entry_columns[k], i) for i in range(SUB) for k in range(i, SUB)}
        near = range(p + 1, min(p + 1 + WINDOW, panels))
        factors = {r: [column(tiles[r], base + k) for k in range(SUB)] for r in near}
        following = [column(tiles[p + 1], base + SUB + k) for k in range(SUB)] if near else []
        own = jnp.where(here, (lane - base == sub).astype(jnp.float32), tiles[p])
        lines = [row(own, k) for k in range(SUB)]
        for r in near:
            tiles[r] = jnp.where(here, 0.0, tiles[r])
        for k in range(SUB):
            inverse_root = lax.rsqrt(entry[k, k])
            coefficient = {i: entry[k, i] * inverse_root for i in range(k + 1, SUB)}
            for i in range(k + 1, SUB):
                for m in range(i, SUB):
                    entry[i, m] = entry[i, m] - coefficient[i] * coefficient[m]
            lines[k] = lines[k] * inverse_root
            for i in range(k + 1, SUB):
                lines[i] = lines[i] - coefficient[i] * lines[k]
            for r in near:
                scaled = factors[r][k] * inverse_root
                for i in range(k + 1, SUB):
                    factors[r][i] = factors[r][i] - coefficient[i] * scaled
                if r == p + 1:
                    for m in range(SUB):
                        following[m] = following[m] - scaled * row(scaled, m)
                tiles[r] = tiles[r] - scaled * lines[k]
        entry_columns = following
        done = lines[SUB - 1]
        for k in range(SUB - 1):
            done = jnp.where(sub == k, lines[k], done)
        work[base : base + SUB, :] = jnp.where(lane < base + SUB, done, 0.0)
        if p + 1 + WINDOW < panels:
            high, middle, low = split_rows(done)
            left = jnp.concatenate([high, high, middle, high, middle, low], axis=0)
            right = jnp.concatenate([high, middle, high, low, middle, high], axis=0)
            update = lax.dot_general(
                left.astype(jnp.bfloat16),
                right.astype(jnp.bfloat16),
                (((0,), (0,)), ((), ())),
                preferred_element_type=jnp.float32,
            )
            for r in range(p + 1 + WINDOW, panels):
                tiles[r] = jnp.where(here, 0.0, tiles[r]) - update[r * SUB : (r + 1) * SUB, :]


def whitener_kernel(
    bank_count, offsets, own, near_ref, rows_ref, same, opposite, mine, other, planes, inner, work,
    near_send, near_receive, keep_sem, show_sem, cross_send, cross_receive, pass_send, pass_receive,
    swap_send, swap_receive, send, receive, local,
):
    pair_rows, half = own.shape
    rows_dev = 2 * pair_rows
    width = 2 * half
    blocks = width // BLOCK
    strips = half // BLOCK
    piece = pair_rows // 2
    bank, sibling, partner, diagonal = neighbours()
    feat = lax.axis_index("feat")
    side = feat % 2
    parity = feat // 2
    role = own_role()
    meets_left = jnp.logical_and(role == 0, bank > 0)
    meets_right = jnp.logical_and(role == TOUCH - 1, bank < bank_count - 1)
    meets = jnp.logical_or(meets_left, meets_right)
    met = jnp.where(meets_left, bank - 1, bank + 1)

    def remote(source, target, send_sem, receive_sem, device):
        return pltpu.make_async_remote_copy(
            src_ref=source,
            dst_ref=target,
            send_sem=send_sem,
            recv_sem=receive_sem,
            device_id=device,
            device_id_type=MESH,
        )

    def part(c):
        return pl.ds(pl.multiple_of(c * piece, piece), piece)

    def beside(k, c):
        return remote(
            own.at[part(c), pl.ds(k * BLOCK, BLOCK)],
            same.at[side * strips + k, part(c)],
            near_send.at[k, c],
            near_receive.at[k, c],
            (bank, sibling),
        )

    def keep(k):
        return pltpu.make_async_copy(
            own.at[:, pl.ds(k * BLOCK, BLOCK)], same.at[side * strips + k], keep_sem.at[k]
        )

    def show(k):
        return pltpu.make_async_copy(
            same.at[(1 - side) * strips + k],
            near_ref.at[:, pl.ds(k * BLOCK, BLOCK)],
            show_sem.at[k],
        )

    def crossing(b):
        return remote(
            same.at[b, part(side)],
            opposite.at[b, part(side)],
            cross_send.at[b],
            cross_receive.at[b],
            (bank, partner),
        )

    def passing(b):
        return remote(
            opposite.at[b, part(side)],
            opposite.at[b, part(side)],
            pass_send.at[b],
            pass_receive.at[b],
            (bank, sibling),
        )

    def swap(b):
        span = pl.ds(b * BLOCK, BLOCK), pl.ds(0, (b + 1) * BLOCK)
        return remote(
            mine.at[span], other.at[span], swap_send.at[b], swap_receive.at[b], (met, feat)
        )

    def strip(place, i, device):
        columns = pl.ds(0, (i + 1) * BLOCK)
        return remote(
            planes.at[0, pl.ds(i * BLOCK, BLOCK), columns],
            rows_ref.at[feat, pl.ds(i % strips * BLOCK, BLOCK), columns],
            send.at[place, i % strips],
            receive.at[place, i % strips],
            (bank, device),
        )

    def stay(i):
        columns = pl.ds(0, (i + 1) * BLOCK)
        return pltpu.make_async_copy(
            planes.at[0, pl.ds(i * BLOCK, BLOCK), columns],
            rows_ref.at[feat, pl.ds(i % strips * BLOCK, BLOCK), columns],
            local.at[i % strips],
        )

    barrier = pltpu.get_barrier_semaphore()
    for k in range(strips):
        keep(k).start()
    for device in (sibling, partner, diagonal):
        pl.semaphore_signal(barrier, inc=1, device_id=(bank, device), device_id_type=MESH)

    @pl.when(meets)
    def _():
        pl.semaphore_signal(barrier, inc=1, device_id=(met, feat), device_id_type=MESH)
        pl.semaphore_wait(barrier, 4)

    @pl.when(jnp.logical_not(meets))
    def _():
        pl.semaphore_wait(barrier, 3)

    for k in range(strips):
        beside(k, 1 - side).start()
        beside(k, side).start()

    row_start = bank * rows_dev
    low, high, label = slot_of(offsets, role, row_start, rows_dev)
    left_open = jnp.logical_and(role == 0, offsets[label] < row_start)
    right_open = jnp.logical_and(role == TOUCH - 1, offsets[label + 1] > row_start + rows_dev)
    joined = jnp.logical_or(left_open, right_open)
    count = (offsets[label + 1] - offsets[label]).astype(jnp.float32)
    eye = (
        lax.broadcasted_iota(jnp.int32, (BLOCK, BLOCK), 0)
        == lax.broadcasted_iota(jnp.int32, (BLOCK, BLOCK), 1)
    ).astype(jnp.float32)

    def cross(b):
        k = b % strips
        owns = side == b // strips

        @pl.when(owns)
        def _():
            keep(k).wait()

        @pl.when(jnp.logical_not(owns))
        def _():
            beside(k, side).wait_recv()

        crossing(b).start()

        @pl.when(jnp.logical_not(owns))
        def _():
            beside(k, 1 - side).wait_recv()
            show(k).start()

    def gather(b):
        crossing(b).wait_recv()
        passing(b).start()
        if b + AHEAD < blocks:
            cross(b + AHEAD)
        passing(b).wait_recv()

    def gram(b):
        here = pl.ds(b * BLOCK, BLOCK), pl.ds(0, (b + 1) * BLOCK)
        mine[here] = jnp.zeros((BLOCK, (b + 1) * BLOCK), jnp.float32)
        for source, shift in ((same, parity), (opposite, 1 - parity)):

            @pl.loop(0, 2)
            def _(c):
                row = 2 * (c * piece + lax.broadcasted_iota(jnp.int32, (piece, 1), 0)) + shift
                inside = jnp.logical_and(row >= low, row < high)
                first = source[b, part(c)]
                first = jnp.where(inside, first, jnp.zeros_like(first))
                second = jnp.concatenate([source[k, part(c)] for k in range(b + 1)], axis=1)
                mine[here] += lax.dot_general(
                    first, second, (((0,), (0,)), ((), ())), preferred_element_type=jnp.float32
                )

        @pl.when(meets)
        def _():
            swap(b).start()

    def hand_out(i):
        own_side = 0 if i < strips else 1

        @pl.when(side == own_side)
        def _():
            strip(0, i, partner).start()
            stay(i).start()

        @pl.when(side != own_side)
        def _():
            strip(1, i, diagonal).start()
            strip(2, i, sibling).start()

    for b in range(AHEAD):
        cross(b)
    gather(0)
    gram(0)
    for n in range(3):
        for i in range(blocks - 1):
            planes[n, i * BLOCK : (i + 1) * BLOCK, (i + 1) * BLOCK :] = jnp.zeros(
                (BLOCK, width - (i + 1) * BLOCK), jnp.bfloat16
            )

    def before(i):
        if i + 1 < blocks:
            gather(i + 1)
            gram(i + 1)
        if i == HOLD:
            for k in range(HOLD):
                hand_out(k)

        @pl.when(meets)
        def _():
            swap(i).wait_recv()

        here = pl.ds(i * BLOCK, BLOCK), pl.ds(0, (i + 1) * BLOCK)
        done = i * BLOCK
        total = (mine[here] + jnp.where(joined, other[here], 0.0)) * (1.0 / count)
        square = total[:, done:] + ridge_shift * eye
        if i > 0:
            left = split(total[:, :done])
            inverse = [planes[n, :done, :done] for n in range(3)]
            factor = split(product(left, inverse, 1))
            square = square - product(factor, factor, 1)
            for n, value in enumerate(split(product(factor, inverse, 0))):
                inner[n, :, :done] = value
        work[...] = square

    def after(i):
        done = i * BLOCK
        here = pl.ds(done, BLOCK)
        corner = split(work[...])
        for n in range(3):
            planes[n, here, done : done + BLOCK] = corner[n]
        if i > 0:
            behind = [inner[n, :, :done] for n in range(3)]
            for n, value in enumerate(split(-product(corner, behind, 0))):
                planes[n, here, :done] = value
        if i >= HOLD:
            hand_out(i)

    @pl.loop(0, blocks)
    def _(j):
        for i in range(blocks):

            @pl.when(j == i)
            def _():
                before(i)

        factor_block(work)
        for i in range(blocks):

            @pl.when(j == i)
            def _():
                after(i)

    @pl.when(meets)
    def _():
        for i in range(blocks):
            swap(i).wait_send()

    for b in range(blocks):
        crossing(b).wait_send()
        passing(b).wait_send()
    for k in range(strips):
        beside(k, side).wait_send()
        beside(k, 1 - side).wait_send()
        show(k).wait()

    for own_side in range(2):

        @pl.when(side == own_side)
        def _():
            for i in range(strips):
                kept, others = own_side * strips + i, (1 - own_side) * strips + i
                strip(0, kept, partner).wait_send()
                strip(1, others, diagonal).wait_send()
                strip(2, others, sibling).wait_send()
                stay(kept).wait()
            for i in range(strips):
                kept = own_side * strips + i
                strip(0, kept, partner).wait_recv()
                strip(1, kept, diagonal).wait_recv()
                strip(2, kept, sibling).wait_recv()


def whitener_rows(offsets, own):
    pair_rows, half = own.shape
    width = 2 * half
    blocks, strips = width // BLOCK, half // BLOCK
    anywhere = pl.BlockSpec(memory_space=pl.ANY)
    dma = pltpu.SemaphoreType.DMA
    return pl.pallas_call(
        functools.partial(whitener_kernel, lax.axis_size("bank")),
        in_specs=[
            pl.BlockSpec(memory_space=pltpu.SMEM),
            pl.BlockSpec(memory_space=pltpu.HBM),
        ],
        out_specs=[anywhere, anywhere],
        out_shape=[
            jax.ShapeDtypeStruct(own.shape, own.dtype),
            jax.ShapeDtypeStruct((TOUCH, half, width), jnp.bfloat16),
        ],
        scratch_shapes=[
            pltpu.VMEM((blocks, pair_rows, BLOCK), jnp.bfloat16),
            pltpu.VMEM((blocks, pair_rows, BLOCK), jnp.bfloat16),
            pltpu.VMEM((width, width), jnp.float32),
            pltpu.VMEM((width, width), jnp.float32),
            pltpu.VMEM((3, width, width), jnp.bfloat16),
            pltpu.VMEM((3, BLOCK, width), jnp.bfloat16),
            pltpu.VMEM((BLOCK, BLOCK), jnp.float32),
            dma((strips, 2)),
            dma((strips, 2)),
            dma((strips,)),
            dma((strips,)),
            dma((blocks,)),
            dma((blocks,)),
            dma((blocks,)),
            dma((blocks,)),
            dma((blocks,)),
            dma((blocks,)),
            dma((3, strips)),
            dma((3, strips)),
            dma((strips,)),
        ],
        compiler_params=pltpu.CompilerParams(
            collective_id=0, has_side_effects=True, vmem_limit_bytes=40 << 20
        ),
    )(offsets, own)


def whiten_kernel(offsets, own, near, factor_ref, out_ref, factors, total, bounds):
    step = pl.program_id(0)
    block_pairs, half = own.shape
    rows_dev = pl.num_programs(0) * block_pairs * 2
    bank, feat = lax.axis_index("bank"), lax.axis_index("feat")
    start = step * block_pairs * 2

    @pl.when(step == 0)
    def _():
        shape = factor_ref.shape[1:]
        row = (feat % 2) * half + lax.broadcasted_iota(jnp.int32, shape, 0)
        inside = lax.broadcasted_iota(jnp.int32, shape, 1) <= row
        for role in range(TOUCH):
            bounds[role], bounds[TOUCH + role], _ = slot_of(
                offsets, jnp.int32(role), bank * rows_dev, rows_dev
            )
        for place in range(TOUCH):
            rows = factor_ref[place]
            factors[place] = jnp.where(inside, rows, jnp.zeros_like(rows))

    total[...] = jnp.zeros_like(total)
    for role in range(TOUCH):
        low, high = bounds[role], bounds[TOUCH + role]

        @pl.when(jnp.logical_and(start < high, start + 2 * block_pairs > low))
        def _():
            place = jnp.where(bank % 2 == 0, role, TOUCH - 1 - role)
            row = start + feat // 2 + 2 * lax.broadcasted_iota(jnp.int32, (block_pairs, 1), 0)
            data = ordered(own[...], near[...], feat % 2 == 1)
            keep = jnp.logical_and(row >= low, row < high)
            data = jnp.where(keep, data, jnp.zeros_like(data))
            total[...] += lax.dot_general(
                data, factors[place], (((1,), (1,)), ((), ())), preferred_element_type=jnp.float32
            )

    out_ref[...] = total[...].astype(jnp.bfloat16)


def whiten(offsets, own, near, factor_rows):
    pair_rows, half = own.shape
    block_pairs = min(256, pair_rows)
    block = pl.BlockSpec((block_pairs, half), lambda i: (i, 0))
    return pl.pallas_call(
        whiten_kernel,
        grid=(pair_rows // block_pairs,),
        in_specs=[
            pl.BlockSpec(memory_space=pltpu.SMEM),
            block,
            block,
            pl.BlockSpec(factor_rows.shape, lambda i: (0, 0, 0)),
        ],
        out_specs=block,
        out_shape=jax.ShapeDtypeStruct((pair_rows, half), jnp.bfloat16),
        scratch_shapes=[
            pltpu.VMEM(factor_rows.shape, jnp.bfloat16),
            pltpu.VMEM((block_pairs, half), jnp.float32),
            pltpu.SMEM((2 * TOUCH,), jnp.int32),
        ],
        compiler_params=pltpu.CompilerParams(vmem_limit_bytes=32 << 20),
    )(offsets, own, near, factor_rows)


def shards(bank_rows, offsets):
    near, factor_rows = whitener_rows(offsets, bank_rows)
    return whiten(offsets, bank_rows, near, factor_rows)


def solution(mesh):
    return jax.shard_map(
        shards,
        mesh=mesh,
        in_specs=(P("bank", "feat"), P()),
        out_specs=P("bank", "feat"),
        check_vma=False,
    )
```

```python
import functools

import jax
import jax.numpy as jnp
from jax import lax
from jax.experimental import pallas as pl
from jax.experimental.pallas import tpu as pltpu
from jax.sharding import PartitionSpec as P

TOUCH = 4
BLOCK = 128
SUB = 8
WINDOW = 4
ridge_shift = 0.5


MESH = pl.DeviceIdType.MESH
AHEAD = 2
HOLD = 4
MOST = 1920


def slot_of(offsets, role, row_start, rows_dev):
    clusters = offsets.shape[0] - 1

    def count(k, found):
        bound = offsets[k]
        first, last = found
        first = first + (bound < row_start).astype(jnp.int32)
        last = last + (bound <= row_start + rows_dev - 1).astype(jnp.int32)
        return first, last

    first, last = lax.fori_loop(1, clusters, count, (jnp.int32(0), jnp.int32(0)))
    middles = last - first - 1
    leading = offsets[first + 1] - row_start
    trailing = row_start + rows_dev - offsets[last]
    early = leading <= trailing
    label = jnp.where(role == 1, first + 1, last - 1)
    label = jnp.where(role == 0, first, jnp.where(role == TOUCH - 1, last, label))
    label = jnp.clip(label, 0, clusters - 1)
    lone = jnp.logical_and(middles == 1, early == (role == 1))
    used = jnp.logical_or(middles == 2, lone)
    used = jnp.logical_or(used, jnp.logical_or(role == 0, role == TOUCH - 1))
    low = jnp.clip(offsets[label] - row_start, 0, rows_dev)
    high = jnp.clip(offsets[label + 1] - row_start, 0, rows_dev)
    return low, jnp.where(used, high, low), label


def own_role():
    feat = lax.axis_index("feat")
    return jnp.where(lax.axis_index("bank") % 2 == 0, feat, TOUCH - 1 - feat)


def neighbours():
    bank, feat = lax.axis_index("bank"), lax.axis_index("feat")
    sibling = feat + 1 - 2 * (feat % 2)
    return bank, sibling, (feat + 2) % TOUCH, (sibling + 2) % TOUCH


def ordered(first, second, swap):
    left = jnp.where(swap, second, first)
    right = jnp.where(swap, first, second)
    return jnp.concatenate([left, right], axis=1)


def split(value):
    high = value.astype(jnp.bfloat16)
    rest = value - high.astype(jnp.float32)
    middle = rest.astype(jnp.bfloat16)
    low = (rest - middle.astype(jnp.float32)).astype(jnp.bfloat16)
    return high, middle, low


def product(left, right, right_dim):
    first = jnp.concatenate([left[n] for n in (0, 0, 1, 0, 1, 2)], axis=1)
    second = jnp.concatenate([right[n] for n in (0, 1, 0, 2, 1, 0)], axis=right_dim)
    return lax.dot_general(
        first, second, (((1,), (right_dim,)), ((), ())), preferred_element_type=jnp.float32
    )


def split_rows(value):
    high = value.astype(jnp.bfloat16).astype(jnp.float32)
    rest = value - high
    middle = rest.astype(jnp.bfloat16).astype(jnp.float32)
    low = (rest - middle).astype(jnp.bfloat16).astype(jnp.float32)
    return high, middle, low


def factor_block(work):
    panels = BLOCK // SUB
    shape = (SUB, BLOCK)
    lane = lax.broadcasted_iota(jnp.int32, shape, 1)
    sub = lax.broadcasted_iota(jnp.int32, shape, 0)

    def column(tile, c):
        return jnp.broadcast_to(tile[:, c : c + 1], shape)

    def row(tile, i):
        return jnp.broadcast_to(tile[i : i + 1, :], shape)

    tiles = [work[p * SUB : (p + 1) * SUB, :] for p in range(panels)]
    entry_columns = [column(tiles[0], k) for k in range(SUB)]
    for p in range(panels):
        base = p * SUB
        here = jnp.logical_and(lane >= base, lane < base + SUB)
        entry = {(i, k): row(entry_columns[k], i) for i in range(SUB) for k in range(i, SUB)}
        near = range(p + 1, min(p + 1 + WINDOW, panels))
        factors = {r: [column(tiles[r], base + k) for k in range(SUB)] for r in near}
        following = [column(tiles[p + 1], base + SUB + k) for k in range(SUB)] if near else []
        own = jnp.where(here, (lane - base == sub).astype(jnp.float32), tiles[p])
        lines = [row(own, k) for k in range(SUB)]
        for r in near:
            tiles[r] = jnp.where(here, 0.0, tiles[r])
        for k in range(SUB):
            inverse_root = lax.rsqrt(entry[k, k])
            coefficient = {i: entry[k, i] * inverse_root for i in range(k + 1, SUB)}
            for i in range(k + 1, SUB):
                for m in range(i, SUB):
                    entry[i, m] = entry[i, m] - coefficient[i] * coefficient[m]
            lines[k] = lines[k] * inverse_root
            for i in range(k + 1, SUB):
                lines[i] = lines[i] - coefficient[i] * lines[k]
            for r in near:
                scaled = factors[r][k] * inverse_root
                for i in range(k + 1, SUB):
                    factors[r][i] = factors[r][i] - coefficient[i] * scaled
                if r == p + 1:
                    for m in range(SUB):
                        following[m] = following[m] - scaled * row(scaled, m)
                tiles[r] = tiles[r] - scaled * lines[k]
        entry_columns = following
        done = lines[SUB - 1]
        for k in range(SUB - 1):
            done = jnp.where(sub == k, lines[k], done)
        work[base : base + SUB, :] = jnp.where(lane < base + SUB, done, 0.0)
        if p + 1 + WINDOW < panels:
            high, middle, low = split_rows(done)
            left = jnp.concatenate([high, high, middle, high, middle, low], axis=0)
            right = jnp.concatenate([high, middle, high, low, middle, high], axis=0)
            update = lax.dot_general(
                left.astype(jnp.bfloat16),
                right.astype(jnp.bfloat16),
                (((0,), (0,)), ((), ())),
                preferred_element_type=jnp.float32,
            )
            for r in range(p + 1 + WINDOW, panels):
                tiles[r] = jnp.where(here, 0.0, tiles[r]) - update[r * SUB : (r + 1) * SUB, :]


def whitener_kernel(
    bank_count, offsets, own, near_ref, rows_ref, same, opposite, same_mask, opposite_mask, mine, other, planes, inner, final,
    work, near_send, near_receive, keep_sem, show_sem, cross_send, cross_receive, pass_send, pass_receive,
    swap_send, swap_receive, send, receive, local, relay_send,
    relay_receive,
):
    pair_rows, half = own.shape
    rows_dev = 2 * pair_rows
    width = 2 * half
    blocks = width // BLOCK
    strips = half // BLOCK
    skip = (rows_dev - MOST) // 4
    piece = (pair_rows - skip) // 2
    bank, sibling, partner, diagonal = neighbours()
    feat = lax.axis_index("feat")
    side = feat % 2
    parity = feat // 2
    role = own_role()
    meets_left = jnp.logical_and(role == 0, bank > 0)
    meets_right = jnp.logical_and(role == TOUCH - 1, bank < bank_count - 1)
    meets = jnp.logical_or(meets_left, meets_right)
    met = jnp.where(meets_left, bank - 1, bank + 1)
    early = role < 2
    needs = jnp.where(early, 0, skip)
    relays = jnp.where(early, bank < bank_count - 1, bank > 0)
    beyond = jnp.where(early, bank + 1, bank - 1)
    end = jnp.where(feat < 2, TOUCH - 1, 0)
    end_is_partner = jnp.logical_or(feat == 1, feat == 2)

    def remote(source, target, send_sem, receive_sem, device):
        return pltpu.make_async_remote_copy(
            src_ref=source,
            dst_ref=target,
            send_sem=send_sem,
            recv_sem=receive_sem,
            device_id=device,
            device_id_type=MESH,
        )

    def part(base, c):
        return pl.ds(pl.multiple_of(base + c * piece, 16), piece)

    def beside(k, holder):
        return remote(
            own.at[:, pl.ds(k * BLOCK, BLOCK)],
            same.at[holder * strips + k],
            near_send.at[k],
            near_receive.at[k],
            (bank, sibling),
        )

    def keep(k):
        return pltpu.make_async_copy(
            own.at[:, pl.ds(k * BLOCK, BLOCK)], same.at[side * strips + k], keep_sem.at[k]
        )

    def show(k):
        return pltpu.make_async_copy(
            same.at[(1 - side) * strips + k],
            near_ref.at[:, pl.ds(k * BLOCK, BLOCK)],
            show_sem.at[k],
        )

    def crossing(b, base=0):
        return remote(
            same.at[b, part(base, side)],
            opposite.at[b, part(0, side)],
            cross_send.at[b],
            cross_receive.at[b],
            (bank, partner),
        )

    def passing(b):
        return remote(
            opposite.at[b, part(0, side)],
            opposite.at[b, part(0, side)],
            pass_send.at[b],
            pass_receive.at[b],
            (bank, sibling),
        )

    def swap(b):
        span = pl.ds(b * BLOCK, BLOCK), pl.ds(0, (b + 1) * BLOCK)
        return remote(
            mine.at[span], other.at[span], swap_send.at[b], swap_receive.at[b], (met, feat)
        )

    def strip(place, i, device, span, slot=feat):
        columns = pl.ds(span[0], span[1] - span[0])
        return remote(
            final.at[i, columns],
            rows_ref.at[slot, i % strips, columns],
            send.at[place, i % strips],
            receive.at[place, i % strips],
            (bank, device),
        )

    def relay(i, span):
        place = rows_ref.at[end, i % strips, pl.ds(span[0], span[1] - span[0])]
        return remote(
            place, place, relay_send.at[i % strips], relay_receive.at[i % strips], (beyond, feat)
        )

    def spans(i):
        whole = (0, i + 1)
        cut = (i + 2) // 2 if i % 4 != 2 else i // 2
        return whole, (0, cut), (cut, i + 1)

    def stay(i):
        columns = pl.ds(0, i + 1)
        return pltpu.make_async_copy(
            final.at[i, columns], rows_ref.at[feat, i % strips, columns], local.at[i % strips]
        )

    barrier = pltpu.get_barrier_semaphore()
    for k in range(strips):
        keep(k).start()
    for device in (sibling, partner, diagonal):
        pl.semaphore_signal(barrier, inc=1, device_id=(bank, device), device_id_type=MESH)

    @pl.when(meets)
    def _():
        pl.semaphore_signal(barrier, inc=1, device_id=(met, feat), device_id_type=MESH)

    @pl.when(relays)
    def _():
        pl.semaphore_signal(barrier, inc=1, device_id=(beyond, feat), device_id_type=MESH)

    pl.semaphore_wait(barrier, 3 + jnp.where(meets, 1, 0) + jnp.where(relays, 1, 0))

    for k in range(strips):
        beside(k, side).start()

    row_start = bank * rows_dev
    low, high, label = slot_of(offsets, role, row_start, rows_dev)
    count = (offsets[label + 1] - offsets[label]).astype(jnp.float32)
    eye = (
        lax.broadcasted_iota(jnp.int32, (BLOCK, BLOCK), 0)
        == lax.broadcasted_iota(jnp.int32, (BLOCK, BLOCK), 1)
    ).astype(jnp.float32)
    for mask, base, shift in ((same_mask, 0, parity), (opposite_mask, needs, 1 - parity)):
        row = 2 * (base + lax.broadcasted_iota(jnp.int32, mask.shape, 0)) + shift
        inside = jnp.logical_and(row >= low, row < high)
        mask[...] = inside.astype(jnp.bfloat16)

    def cross(b):
        k = b % strips
        owns = side == b // strips

        @pl.when(owns)
        def _():
            keep(k).wait()

        @pl.when(jnp.logical_not(owns))
        def _():
            beside(k, 1 - side).wait_recv()
            show(k).start()

        @pl.when(early)
        def _():
            crossing(b, skip).start()

        @pl.when(jnp.logical_not(early))
        def _():
            crossing(b).start()

    def gather(b):
        crossing(b).wait_recv()
        passing(b).start()
        if b + AHEAD < blocks:
            cross(b + AHEAD)
        passing(b).wait_recv()

    def gram(b):
        here = pl.ds(b * BLOCK, BLOCK), pl.ds(0, (b + 1) * BLOCK)
        mine[here] = jnp.zeros((BLOCK, (b + 1) * BLOCK), jnp.float32)
        for source, mask in ((same, same_mask), (opposite, opposite_mask)):
            rows = mask.shape[0] // 2

            @pl.loop(0, 2)
            def _(c):
                span = pl.ds(pl.multiple_of(c * rows, rows), rows)
                first = source[b, span] * mask[span]
                second = jnp.concatenate([source[k, span] for k in range(b + 1)], axis=1)
                mine[here] += lax.dot_general(
                    first, second, (((0,), (0,)), ((), ())), preferred_element_type=jnp.float32
                )

        @pl.when(meets)
        def _():
            swap(b).start()

    choices = (jnp.logical_not(meets), meets_right, meets_left)
    end_choices = (
        jnp.logical_not(relays),
        jnp.logical_and(relays, early),
        jnp.logical_and(relays, jnp.logical_not(early)),
    )

    def hand_out(i):
        own_side = 0 if i < strips else 1

        whole = spans(i)[0]
        for choice, span in zip(choices, spans(i)):
            if span[0] < span[1]:

                @pl.when(jnp.logical_and(choice, side == own_side))
                def _():
                    strip(0, i, partner, span).start()

                @pl.when(jnp.logical_and(choice, side != own_side))
                def _():
                    strip(1, i, diagonal, span).start()

        @pl.when(side == own_side)
        def _():
            stay(i).start()

        @pl.when(side != own_side)
        def _():
            strip(2, i, sibling, whole).start()

    for b in range(AHEAD):
        cross(b)
    gather(0)
    gram(0)
    for n in range(3):
        for i in range(blocks - 1):
            planes[n, i * BLOCK : (i + 1) * BLOCK, (i + 1) * BLOCK :] = jnp.zeros(
                (BLOCK, width - (i + 1) * BLOCK), jnp.bfloat16
            )

    def before(i):
        if i + 1 < blocks:
            gather(i + 1)
            gram(i + 1)
        if i == HOLD:
            for k in range(HOLD):
                hand_out(k)

        @pl.when(meets)
        def _():
            swap(i).wait_recv()

        here = pl.ds(i * BLOCK, BLOCK), pl.ds(0, (i + 1) * BLOCK)
        done = i * BLOCK
        total = (mine[here] + jnp.where(meets, other[here], 0.0)) * (1.0 / count)
        square = total[:, done:] + ridge_shift * eye
        if i > 0:
            left = split(total[:, :done])
            inverse = [planes[n, :done, :done] for n in range(3)]
            factor = split(product(left, inverse, 1))
            square = square - product(factor, factor, 1)
            for n, value in enumerate(split(product(factor, inverse, 0))):
                inner[n, :, :done] = value
        work[...] = square

    def after(i):
        done = i * BLOCK
        here = pl.ds(done, BLOCK)
        corner = split(work[...])
        for n in range(3):
            planes[n, here, done : done + BLOCK] = corner[n]
        final[i, i] = corner[0]
        if i > 0:
            behind = [inner[n, :, :done] for n in range(3)]
            for n, value in enumerate(split(-product(corner, behind, 0))):
                planes[n, here, :done] = value
                for k in range(i if n == 0 else 0):
                    final[i, k] = value[:, k * BLOCK : (k + 1) * BLOCK]
        if i >= HOLD:
            hand_out(i)

    @pl.loop(0, blocks)
    def _(j):
        for i in range(blocks):

            @pl.when(j == i)
            def _():
                before(i)

        factor_block(work)
        for i in range(blocks):

            @pl.when(j == i)
            def _():
                after(i)

    for own_side in range(2):
        for i in range(own_side * strips, own_side * strips + strips):
            whole, front, back = spans(i)
            for choice, span, rest in zip(end_choices, (whole, front, back), (None, back, front)):
                for place, is_end in ((0, end_is_partner), (1, jnp.logical_not(end_is_partner))):
                    at_end = jnp.logical_and(side == own_side, is_end)

                    @pl.when(jnp.logical_and(choice, at_end))
                    def _():
                        if span[0] < span[1]:
                            strip(place, i, partner, span, end).wait_recv()
                            if rest is not None:
                                relay(i, span).start()
                        middle = (diagonal, partner)[place]
                        strip(1 - place, i, partner, whole, middle).wait_recv()

        @pl.when(side == own_side)
        def _():
            for i in range(own_side * strips, own_side * strips + strips):
                strip(2, i, sibling, spans(i)[0], sibling).wait_recv()
                stay(i).wait()

    for own_side in range(2):
        for i in range(own_side * strips, own_side * strips + strips):
            whole, front, back = spans(i)
            for choice, span, rest in zip(end_choices[1:], (front, back), (back, front)):

                @pl.when(jnp.logical_and(choice, side == own_side))
                def _():
                    if rest[0] < rest[1]:
                        relay(i, rest).wait_recv()
                    if span[0] < span[1]:
                        relay(i, span).wait_send()

    @pl.when(meets)
    def _():
        for i in range(blocks):
            swap(i).wait_send()

    for b in range(blocks):
        crossing(b).wait_send()
        passing(b).wait_send()
    for k in range(strips):
        beside(k, side).wait_send()
        show(k).wait()
    for i in range(blocks):
        own_side = i // strips
        whole = spans(i)[0]
        for choice, span in zip(choices, spans(i)):
            if span[0] < span[1]:

                @pl.when(jnp.logical_and(choice, side == own_side))
                def _():
                    strip(0, i, partner, span).wait_send()

                @pl.when(jnp.logical_and(choice, side != own_side))
                def _():
                    strip(1, i, diagonal, span).wait_send()

        @pl.when(side != own_side)
        def _():
            strip(2, i, sibling, whole).wait_send()


def whitener_rows(offsets, own):
    pair_rows, half = own.shape
    width = 2 * half
    blocks, strips = width // BLOCK, half // BLOCK
    window = pair_rows - (2 * pair_rows - MOST) // 4
    anywhere = pl.BlockSpec(memory_space=pl.ANY)
    dma = pltpu.SemaphoreType.DMA
    return pl.pallas_call(
        functools.partial(whitener_kernel, lax.axis_size("bank")),
        in_specs=[
            pl.BlockSpec(memory_space=pltpu.SMEM),
            pl.BlockSpec(memory_space=pltpu.HBM),
        ],
        out_specs=[anywhere, anywhere],
        out_shape=[
            jax.ShapeDtypeStruct(own.shape, own.dtype),
            jax.ShapeDtypeStruct((TOUCH, strips, blocks, BLOCK, BLOCK), jnp.bfloat16),
        ],
        scratch_shapes=[
            pltpu.VMEM((blocks, pair_rows, BLOCK), jnp.bfloat16),
            pltpu.VMEM((blocks, window, BLOCK), jnp.bfloat16),
            pltpu.VMEM((pair_rows, BLOCK), jnp.bfloat16),
            pltpu.VMEM((window, BLOCK), jnp.bfloat16),
            pltpu.VMEM((width, width), jnp.float32),
            pltpu.VMEM((width, width), jnp.float32),
            pltpu.VMEM((3, width, width), jnp.bfloat16),
            pltpu.VMEM((3, BLOCK, width), jnp.bfloat16),
            pltpu.VMEM((blocks, blocks, BLOCK, BLOCK), jnp.bfloat16),
            pltpu.VMEM((BLOCK, BLOCK), jnp.float32),
            dma((strips,)),
            dma((strips,)),
            dma((strips,)),
            dma((strips,)),
            dma((blocks,)),
            dma((blocks,)),
            dma((blocks,)),
            dma((blocks,)),
            dma((blocks,)),
            dma((blocks,)),
            dma((3, strips)),
            dma((3, strips)),
            dma((strips,)),
            dma((strips,)),
            dma((strips,)),
        ],
        compiler_params=pltpu.CompilerParams(
            collective_id=0, has_side_effects=True, vmem_limit_bytes=40 << 20
        ),
    )(offsets, own)


def whiten_kernel(offsets, own, near, factor_ref, out_ref, factors, total, bounds):
    step = pl.program_id(0)
    block_pairs, half = own.shape
    rows_dev = pl.num_programs(0) * block_pairs * 2
    bank, feat = lax.axis_index("bank"), lax.axis_index("feat")
    start = step * block_pairs * 2

    @pl.when(step == 0)
    def _():
        strips, blocks = factor_ref.shape[1:3]
        lead = lax.broadcasted_iota(jnp.int32, (BLOCK, BLOCK), 0) - lax.broadcasted_iota(
            jnp.int32, (BLOCK, BLOCK), 1
        )
        for role in range(TOUCH):
            bounds[role], bounds[TOUCH + role], _ = slot_of(
                offsets, jnp.int32(role), bank * rows_dev, rows_dev
            )
        for i in range(strips):
            for k in range(blocks):
                inside = lead + (feat % 2) * half + (i - k) * BLOCK >= 0
                for place in range(TOUCH):
                    rows = factor_ref[place, i, k]
                    factors[place, i * BLOCK : (i + 1) * BLOCK, k * BLOCK : (k + 1) * BLOCK] = (
                        jnp.where(inside, rows, jnp.zeros_like(rows))
                    )

    total[...] = jnp.zeros_like(total)
    for role in range(TOUCH):
        low, high = bounds[role], bounds[TOUCH + role]

        @pl.when(jnp.logical_and(start < high, start + 2 * block_pairs > low))
        def _():
            place = jnp.where(bank % 2 == 0, role, TOUCH - 1 - role)
            row = start + feat // 2 + 2 * lax.broadcasted_iota(jnp.int32, (block_pairs, 1), 0)
            data = ordered(own[...], near[...], feat % 2 == 1)
            keep = jnp.logical_and(row >= low, row < high)
            data = jnp.where(keep, data, jnp.zeros_like(data))
            total[...] += lax.dot_general(
                data, factors[place], (((1,), (1,)), ((), ())), preferred_element_type=jnp.float32
            )

    out_ref[...] = total[...].astype(jnp.bfloat16)


def whiten(offsets, own, near, factor_rows):
    pair_rows, half = own.shape
    block_pairs = min(256, pair_rows)
    block = pl.BlockSpec((block_pairs, half), lambda i: (i, 0))
    return pl.pallas_call(
        whiten_kernel,
        grid=(pair_rows // block_pairs,),
        in_specs=[
            pl.BlockSpec(memory_space=pltpu.SMEM),
            block,
            block,
            pl.BlockSpec(factor_rows.shape, lambda i: (0, 0, 0, 0, 0)),
        ],
        out_specs=block,
        out_shape=jax.ShapeDtypeStruct((pair_rows, half), jnp.bfloat16),
        scratch_shapes=[
            pltpu.VMEM((TOUCH, half, 2 * half), jnp.bfloat16),
            pltpu.VMEM((block_pairs, half), jnp.float32),
            pltpu.SMEM((2 * TOUCH,), jnp.int32),
        ],
        compiler_params=pltpu.CompilerParams(vmem_limit_bytes=32 << 20),
    )(offsets, own, near, factor_rows)


def shards(bank_rows, offsets):
    near, factor_rows = whitener_rows(offsets, bank_rows)
    return whiten(offsets, bank_rows, near, factor_rows)


def solution(mesh):
    return jax.shard_map(
        shards,
        mesh=mesh,
        in_specs=(P("bank", "feat"), P()),
        out_specs=P("bank", "feat"),
        check_vma=False,
    )
```

```python
import functools

import jax
import jax.numpy as jnp
from jax import lax
from jax.experimental import pallas as pl
from jax.experimental.pallas import tpu as pltpu
from jax.sharding import PartitionSpec as P

TOUCH = 4
BLOCK = 128
SUB = 8
WINDOW = 4
ridge_shift = 0.5


MESH = pl.DeviceIdType.MESH
AHEAD = 2
HOLD = 4
MOST = 1920


def slot_of(offsets, role, row_start, rows_dev):
    clusters = offsets.shape[0] - 1

    def count(k, found):
        bound = offsets[k]
        first, last = found
        first = first + (bound < row_start).astype(jnp.int32)
        last = last + (bound <= row_start + rows_dev - 1).astype(jnp.int32)
        return first, last

    first, last = lax.fori_loop(1, clusters, count, (jnp.int32(0), jnp.int32(0)))
    middles = last - first - 1
    leading = offsets[first + 1] - row_start
    trailing = row_start + rows_dev - offsets[last]
    early = leading <= trailing
    label = jnp.where(role == 1, first + 1, last - 1)
    label = jnp.where(role == 0, first, jnp.where(role == TOUCH - 1, last, label))
    label = jnp.clip(label, 0, clusters - 1)
    lone = jnp.logical_and(middles == 1, early == (role == 1))
    used = jnp.logical_or(middles == 2, lone)
    used = jnp.logical_or(used, jnp.logical_or(role == 0, role == TOUCH - 1))
    low = jnp.clip(offsets[label] - row_start, 0, rows_dev)
    high = jnp.clip(offsets[label + 1] - row_start, 0, rows_dev)
    return low, jnp.where(used, high, low), label


def own_role():
    feat = lax.axis_index("feat")
    return jnp.where(lax.axis_index("bank") % 2 == 0, feat, TOUCH - 1 - feat)


def neighbours():
    bank, feat = lax.axis_index("bank"), lax.axis_index("feat")
    sibling = feat + 1 - 2 * (feat % 2)
    return bank, sibling, (feat + 2) % TOUCH, (sibling + 2) % TOUCH


def split(value):
    high = value.astype(jnp.bfloat16)
    rest = value - high.astype(jnp.float32)
    middle = rest.astype(jnp.bfloat16)
    low = (rest - middle.astype(jnp.float32)).astype(jnp.bfloat16)
    return high, middle, low


def product(left, right, right_dim):
    first = jnp.concatenate([left[n] for n in (0, 0, 1, 0, 1, 2)], axis=1)
    second = jnp.concatenate([right[n] for n in (0, 1, 0, 2, 1, 0)], axis=right_dim)
    return lax.dot_general(
        first, second, (((1,), (right_dim,)), ((), ())), preferred_element_type=jnp.float32
    )


def split_rows(value):
    high = value.astype(jnp.bfloat16).astype(jnp.float32)
    rest = value - high
    middle = rest.astype(jnp.bfloat16).astype(jnp.float32)
    low = (rest - middle).astype(jnp.bfloat16).astype(jnp.float32)
    return high, middle, low


def factor_block(work):
    panels = BLOCK // SUB
    shape = (SUB, BLOCK)
    lane = lax.broadcasted_iota(jnp.int32, shape, 1)
    sub = lax.broadcasted_iota(jnp.int32, shape, 0)

    def column(tile, c):
        return jnp.broadcast_to(tile[:, c : c + 1], shape)

    def row(tile, i):
        return jnp.broadcast_to(tile[i : i + 1, :], shape)

    tiles = [work[p * SUB : (p + 1) * SUB, :] for p in range(panels)]
    entry_columns = [column(tiles[0], k) for k in range(SUB)]
    for p in range(panels):
        base = p * SUB
        here = jnp.logical_and(lane >= base, lane < base + SUB)
        entry = {(i, k): row(entry_columns[k], i) for i in range(SUB) for k in range(i, SUB)}
        near = range(p + 1, min(p + 1 + WINDOW, panels))
        factors = {r: [column(tiles[r], base + k) for k in range(SUB)] for r in near}
        following = [column(tiles[p + 1], base + SUB + k) for k in range(SUB)] if near else []
        own = jnp.where(here, (lane - base == sub).astype(jnp.float32), tiles[p])
        lines = [row(own, k) for k in range(SUB)]
        for r in near:
            tiles[r] = jnp.where(here, 0.0, tiles[r])
        for k in range(SUB):
            inverse_root = lax.rsqrt(entry[k, k])
            coefficient = {i: entry[k, i] * inverse_root for i in range(k + 1, SUB)}
            for i in range(k + 1, SUB):
                for m in range(i, SUB):
                    entry[i, m] = entry[i, m] - coefficient[i] * coefficient[m]
            lines[k] = lines[k] * inverse_root
            for i in range(k + 1, SUB):
                lines[i] = lines[i] - coefficient[i] * lines[k]
            for r in near:
                scaled = factors[r][k] * inverse_root
                for i in range(k + 1, SUB):
                    factors[r][i] = factors[r][i] - coefficient[i] * scaled
                if r == p + 1:
                    for m in range(SUB):
                        following[m] = following[m] - scaled * row(scaled, m)
                tiles[r] = tiles[r] - scaled * lines[k]
        entry_columns = following
        done = lines[SUB - 1]
        for k in range(SUB - 1):
            done = jnp.where(sub == k, lines[k], done)
        work[base : base + SUB, :] = jnp.where(lane < base + SUB, done, 0.0)
        if p + 1 + WINDOW < panels:
            high, middle, low = split_rows(done)
            left = jnp.concatenate([high, high, middle, high, middle, low], axis=0)
            right = jnp.concatenate([high, middle, high, low, middle, high], axis=0)
            update = lax.dot_general(
                left.astype(jnp.bfloat16),
                right.astype(jnp.bfloat16),
                (((0,), (0,)), ((), ())),
                preferred_element_type=jnp.float32,
            )
            for r in range(p + 1 + WINDOW, panels):
                tiles[r] = jnp.where(here, 0.0, tiles[r]) - update[r * SUB : (r + 1) * SUB, :]


def whitener_kernel(
    bank_count, offsets, own, near_ref, rows_ref, same, opposite, same_mask, opposite_mask, mine, other, planes, inner, final,
    work, near_send, near_receive, keep_sem, show_sem, cross_send, cross_receive, pass_send, pass_receive,
    swap_send, swap_receive, send, receive, local, relay_send,
    relay_receive,
):
    pair_rows, half = own.shape
    rows_dev = 2 * pair_rows
    width = 2 * half
    blocks = width // BLOCK
    strips = half // BLOCK
    skip = (rows_dev - MOST) // 4
    piece = (pair_rows - skip) // 2
    bank, sibling, partner, diagonal = neighbours()
    feat = lax.axis_index("feat")
    side = feat % 2
    parity = feat // 2
    role = own_role()
    meets_left = jnp.logical_and(role == 0, bank > 0)
    meets_right = jnp.logical_and(role == TOUCH - 1, bank < bank_count - 1)
    meets = jnp.logical_or(meets_left, meets_right)
    met = jnp.where(meets_left, bank - 1, bank + 1)
    early = role < 2
    needs = jnp.where(early, 0, skip)
    relays = jnp.where(early, bank < bank_count - 1, bank > 0)
    beyond = jnp.where(early, bank + 1, bank - 1)
    end = jnp.where(feat < 2, TOUCH - 1, 0)
    end_is_partner = jnp.logical_or(feat == 1, feat == 2)

    def remote(source, target, send_sem, receive_sem, device):
        return pltpu.make_async_remote_copy(
            src_ref=source,
            dst_ref=target,
            send_sem=send_sem,
            recv_sem=receive_sem,
            device_id=device,
            device_id_type=MESH,
        )

    def part(base, c):
        return pl.ds(pl.multiple_of(base + c * piece, 16), piece)

    def beside(k, holder):
        return remote(
            own.at[:, pl.ds(k * BLOCK, BLOCK)],
            same.at[holder * strips + k],
            near_send.at[k],
            near_receive.at[k],
            (bank, sibling),
        )

    def keep(k):
        return pltpu.make_async_copy(
            own.at[:, pl.ds(k * BLOCK, BLOCK)], same.at[side * strips + k], keep_sem.at[k]
        )

    def show(k):
        return pltpu.make_async_copy(
            same.at[(1 - side) * strips + k],
            near_ref.at[:, pl.ds(k * BLOCK, BLOCK)],
            show_sem.at[k],
        )

    def crossing(b, base=0):
        return remote(
            same.at[b, part(base, side)],
            opposite.at[b, part(0, side)],
            cross_send.at[b],
            cross_receive.at[b],
            (bank, partner),
        )

    def passing(b):
        return remote(
            opposite.at[b, part(0, side)],
            opposite.at[b, part(0, side)],
            pass_send.at[b],
            pass_receive.at[b],
            (bank, sibling),
        )

    def swap(b):
        span = pl.ds(b * BLOCK, BLOCK), pl.ds(0, (b + 1) * BLOCK)
        return remote(
            mine.at[span], other.at[span], swap_send.at[b], swap_receive.at[b], (met, feat)
        )

    def strip(place, i, device, span, slot=feat):
        columns = pl.ds(span[0], span[1] - span[0])
        return remote(
            final.at[i, columns],
            rows_ref.at[slot, i % strips, columns],
            send.at[place, i % strips],
            receive.at[place, i % strips],
            (bank, device),
        )

    def relay(i, span):
        place = rows_ref.at[end, i % strips, pl.ds(span[0], span[1] - span[0])]
        return remote(
            place, place, relay_send.at[i % strips], relay_receive.at[i % strips], (beyond, feat)
        )

    def spans(i):
        whole = (0, i + 1)
        cut = (i + 2) // 2 if i % 4 != 2 else i // 2
        return whole, (0, cut), (cut, i + 1)

    def stay(i):
        columns = pl.ds(0, i + 1)
        return pltpu.make_async_copy(
            final.at[i, columns], rows_ref.at[feat, i % strips, columns], local.at[i % strips]
        )

    barrier = pltpu.get_barrier_semaphore()
    for k in range(strips):
        keep(k).start()
    for device in (sibling, partner, diagonal):
        pl.semaphore_signal(barrier, inc=1, device_id=(bank, device), device_id_type=MESH)

    @pl.when(meets)
    def _():
        pl.semaphore_signal(barrier, inc=1, device_id=(met, feat), device_id_type=MESH)

    @pl.when(relays)
    def _():
        pl.semaphore_signal(barrier, inc=1, device_id=(beyond, feat), device_id_type=MESH)

    pl.semaphore_wait(barrier, 3 + jnp.where(meets, 1, 0) + jnp.where(relays, 1, 0))

    for k in range(strips):
        beside(k, side).start()

    row_start = bank * rows_dev
    low, high, label = slot_of(offsets, role, row_start, rows_dev)
    count = (offsets[label + 1] - offsets[label]).astype(jnp.float32)
    eye = (
        lax.broadcasted_iota(jnp.int32, (BLOCK, BLOCK), 0)
        == lax.broadcasted_iota(jnp.int32, (BLOCK, BLOCK), 1)
    ).astype(jnp.float32)
    for mask, base, shift in ((same_mask, 0, parity), (opposite_mask, needs, 1 - parity)):
        row = 2 * (base + lax.broadcasted_iota(jnp.int32, mask.shape, 0)) + shift
        inside = jnp.logical_and(row >= low, row < high)
        mask[...] = inside.astype(jnp.bfloat16)

    def cross(b):
        k = b % strips
        owns = side == b // strips

        @pl.when(owns)
        def _():
            keep(k).wait()

        @pl.when(jnp.logical_not(owns))
        def _():
            beside(k, 1 - side).wait_recv()
            show(k).start()

        @pl.when(early)
        def _():
            crossing(b, skip).start()

        @pl.when(jnp.logical_not(early))
        def _():
            crossing(b).start()

    def gather(b):
        crossing(b).wait_recv()
        passing(b).start()
        if b + AHEAD < blocks:
            cross(b + AHEAD)
        passing(b).wait_recv()

    def gram(b):
        here = pl.ds(b * BLOCK, BLOCK), pl.ds(0, (b + 1) * BLOCK)
        mine[here] = jnp.zeros((BLOCK, (b + 1) * BLOCK), jnp.float32)
        for source, mask in ((same, same_mask), (opposite, opposite_mask)):
            rows = mask.shape[0] // 2

            @pl.loop(0, 2)
            def _(c):
                span = pl.ds(pl.multiple_of(c * rows, rows), rows)
                first = source[b, span] * mask[span]
                second = jnp.concatenate([source[k, span] for k in range(b + 1)], axis=1)
                mine[here] += lax.dot_general(
                    first, second, (((0,), (0,)), ((), ())), preferred_element_type=jnp.float32
                )

        @pl.when(meets)
        def _():
            swap(b).start()

    choices = (jnp.logical_not(meets), meets_right, meets_left)
    end_choices = (
        jnp.logical_not(relays),
        jnp.logical_and(relays, early),
        jnp.logical_and(relays, jnp.logical_not(early)),
    )

    def hand_out(i):
        own_side = 0 if i < strips else 1

        whole = spans(i)[0]
        for choice, span in zip(choices, spans(i)):
            if span[0] < span[1]:

                @pl.when(jnp.logical_and(choice, side == own_side))
                def _():
                    strip(0, i, partner, span).start()

                @pl.when(jnp.logical_and(choice, side != own_side))
                def _():
                    strip(1, i, diagonal, span).start()

        @pl.when(side == own_side)
        def _():
            stay(i).start()

        @pl.when(side != own_side)
        def _():
            strip(2, i, sibling, whole).start()

    for b in range(AHEAD):
        cross(b)
    gather(0)
    gram(0)
    for n in range(3):
        for i in range(blocks - 1):
            planes[n, i * BLOCK : (i + 1) * BLOCK, (i + 1) * BLOCK :] = jnp.zeros(
                (BLOCK, width - (i + 1) * BLOCK), jnp.bfloat16
            )

    def before(i):
        if i + 1 < blocks:
            gather(i + 1)
            gram(i + 1)
        if i == HOLD:
            for k in range(HOLD):
                hand_out(k)

        @pl.when(meets)
        def _():
            swap(i).wait_recv()

        here = pl.ds(i * BLOCK, BLOCK), pl.ds(0, (i + 1) * BLOCK)
        done = i * BLOCK
        total = (mine[here] + jnp.where(meets, other[here], 0.0)) * (1.0 / count)
        square = total[:, done:] + ridge_shift * eye
        if i > 0:
            left = split(total[:, :done])
            groups = [(k, min(k + 2 * BLOCK, done)) for k in range(0, done, 2 * BLOCK)]
            factor = []
            for start, stop in groups:
                inverse = [planes[n, start:stop, :stop] for n in range(3)]
                factor.append(product([value[:, :stop] for value in left], inverse, 1))
            factor = split(jnp.concatenate(factor, axis=1))
            square = square - product(factor, factor, 1)
            for start, stop in groups:
                inverse = [planes[n, start:done, start:stop] for n in range(3)]
                behind = product([value[:, start:] for value in factor], inverse, 0)
                for n, value in enumerate(split(behind)):
                    inner[n, :, start:stop] = value
        work[...] = square

    def after(i):
        done = i * BLOCK
        here = pl.ds(done, BLOCK)
        corner = split(work[...])
        for n in range(3):
            planes[n, here, done : done + BLOCK] = corner[n]
        final[i, i] = corner[0]
        if i > 0:
            behind = [inner[n, :, :done] for n in range(3)]
            for n, value in enumerate(split(-product(corner, behind, 0))):
                planes[n, here, :done] = value
                for k in range(i if n == 0 else 0):
                    final[i, k] = value[:, k * BLOCK : (k + 1) * BLOCK]
        if i >= HOLD:
            hand_out(i)

    @pl.loop(0, blocks)
    def _(j):
        for i in range(blocks):

            @pl.when(j == i)
            def _():
                before(i)

        factor_block(work)
        for i in range(blocks):

            @pl.when(j == i)
            def _():
                after(i)

    for own_side in range(2):
        for i in range(own_side * strips, own_side * strips + strips):
            whole, front, back = spans(i)
            for choice, span, rest in zip(end_choices, (whole, front, back), (None, back, front)):
                for place, is_end in ((0, end_is_partner), (1, jnp.logical_not(end_is_partner))):
                    at_end = jnp.logical_and(side == own_side, is_end)

                    @pl.when(jnp.logical_and(choice, at_end))
                    def _():
                        if span[0] < span[1]:
                            strip(place, i, partner, span, end).wait_recv()
                            if rest is not None:
                                relay(i, span).start()
                        middle = (diagonal, partner)[place]
                        strip(1 - place, i, partner, whole, middle).wait_recv()

        @pl.when(side == own_side)
        def _():
            for i in range(own_side * strips, own_side * strips + strips):
                strip(2, i, sibling, spans(i)[0], sibling).wait_recv()
                stay(i).wait()

    for own_side in range(2):
        for i in range(own_side * strips, own_side * strips + strips):
            whole, front, back = spans(i)
            for choice, span, rest in zip(end_choices[1:], (front, back), (back, front)):

                @pl.when(jnp.logical_and(choice, side == own_side))
                def _():
                    if rest[0] < rest[1]:
                        relay(i, rest).wait_recv()
                    if span[0] < span[1]:
                        relay(i, span).wait_send()

    @pl.when(meets)
    def _():
        for i in range(blocks):
            swap(i).wait_send()

    for b in range(blocks):
        crossing(b).wait_send()
        passing(b).wait_send()
    for k in range(strips):
        beside(k, side).wait_send()
        show(k).wait()
    for i in range(blocks):
        own_side = i // strips
        whole = spans(i)[0]
        for choice, span in zip(choices, spans(i)):
            if span[0] < span[1]:

                @pl.when(jnp.logical_and(choice, side == own_side))
                def _():
                    strip(0, i, partner, span).wait_send()

                @pl.when(jnp.logical_and(choice, side != own_side))
                def _():
                    strip(1, i, diagonal, span).wait_send()

        @pl.when(side != own_side)
        def _():
            strip(2, i, sibling, whole).wait_send()


def whitener_rows(offsets, own):
    pair_rows, half = own.shape
    width = 2 * half
    blocks, strips = width // BLOCK, half // BLOCK
    window = pair_rows - (2 * pair_rows - MOST) // 4
    anywhere = pl.BlockSpec(memory_space=pl.ANY)
    dma = pltpu.SemaphoreType.DMA
    return pl.pallas_call(
        functools.partial(whitener_kernel, lax.axis_size("bank")),
        in_specs=[
            pl.BlockSpec(memory_space=pltpu.SMEM),
            pl.BlockSpec(memory_space=pltpu.HBM),
        ],
        out_specs=[anywhere, anywhere],
        out_shape=[
            jax.ShapeDtypeStruct(own.shape, own.dtype),
            jax.ShapeDtypeStruct((TOUCH, strips, blocks, BLOCK, BLOCK), jnp.bfloat16),
        ],
        scratch_shapes=[
            pltpu.VMEM((blocks, pair_rows, BLOCK), jnp.bfloat16),
            pltpu.VMEM((blocks, window, BLOCK), jnp.bfloat16),
            pltpu.VMEM((pair_rows, BLOCK), jnp.bfloat16),
            pltpu.VMEM((window, BLOCK), jnp.bfloat16),
            pltpu.VMEM((width, width), jnp.float32),
            pltpu.VMEM((width, width), jnp.float32),
            pltpu.VMEM((3, width, width), jnp.bfloat16),
            pltpu.VMEM((3, BLOCK, width), jnp.bfloat16),
            pltpu.VMEM((blocks, blocks, BLOCK, BLOCK), jnp.bfloat16),
            pltpu.VMEM((BLOCK, BLOCK), jnp.float32),
            dma((strips,)),
            dma((strips,)),
            dma((strips,)),
            dma((strips,)),
            dma((blocks,)),
            dma((blocks,)),
            dma((blocks,)),
            dma((blocks,)),
            dma((blocks,)),
            dma((blocks,)),
            dma((3, strips)),
            dma((3, strips)),
            dma((strips,)),
            dma((strips,)),
            dma((strips,)),
        ],
        compiler_params=pltpu.CompilerParams(
            collective_id=0, has_side_effects=True, vmem_limit_bytes=40 << 20
        ),
    )(offsets, own)


def whiten_kernel(offsets, own, near, factor_ref, out_ref, total, bounds):
    step = pl.program_id(0)
    block_pairs, half = own.shape
    strips = half // BLOCK
    rows_dev = pl.num_programs(0) * block_pairs * 2
    bank, feat = lax.axis_index("bank"), lax.axis_index("feat")
    start = step * block_pairs * 2

    @pl.when(step == 0)
    def _():
        for role in range(TOUCH):
            bounds[role], bounds[TOUCH + role], _ = slot_of(
                offsets, jnp.int32(role), bank * rows_dev, rows_dev
            )

    total[...] = jnp.zeros_like(total)
    zero = jnp.zeros((BLOCK, BLOCK), jnp.bfloat16)

    def add(side, low, high, place):
        count = (side + 1) * strips
        row = start + feat // 2 + 2 * lax.broadcasted_iota(jnp.int32, (block_pairs, 1), 0)
        data = own[...] if side == 0 else jnp.concatenate([near[...], own[...]], axis=1)
        keep = jnp.logical_and(row >= low, row < high)
        data = jnp.where(keep, data, jnp.zeros_like(data))
        lines = []
        for i in range(strips):
            last = side * strips + i
            line = [factor_ref[place, i, k] if k <= last else zero for k in range(count)]
            lines.append(jnp.concatenate(line, axis=1))
        total[...] += lax.dot_general(
            data,
            jnp.concatenate(lines, axis=0),
            (((1,), (1,)), ((), ())),
            preferred_element_type=jnp.float32,
        )

    for role in range(TOUCH):
        low, high = bounds[role], bounds[TOUCH + role]
        place = jnp.where(bank % 2 == 0, role, TOUCH - 1 - role)
        inside = jnp.logical_and(start < high, start + 2 * block_pairs > low)
        for side in range(2):

            @pl.when(jnp.logical_and(inside, feat % 2 == side))
            def _():
                add(side, low, high, place)

    out_ref[...] = total[...].astype(jnp.bfloat16)


def whiten(offsets, own, near, factor_rows):
    pair_rows, half = own.shape
    block_pairs = min(256, pair_rows)
    block = pl.BlockSpec((block_pairs, half), lambda i: (i, 0))
    return pl.pallas_call(
        whiten_kernel,
        grid=(pair_rows // block_pairs,),
        in_specs=[
            pl.BlockSpec(memory_space=pltpu.SMEM),
            block,
            block,
            pl.BlockSpec(factor_rows.shape, lambda i: (0, 0, 0, 0, 0)),
        ],
        out_specs=block,
        out_shape=jax.ShapeDtypeStruct((pair_rows, half), jnp.bfloat16),
        scratch_shapes=[
            pltpu.VMEM((block_pairs, half), jnp.float32),
            pltpu.SMEM((2 * TOUCH,), jnp.int32),
        ],
        compiler_params=pltpu.CompilerParams(vmem_limit_bytes=32 << 20),
    )(offsets, own, near, factor_rows)


def shards(bank_rows, offsets):
    near, factor_rows = whitener_rows(offsets, bank_rows)
    return whiten(offsets, bank_rows, near, factor_rows)


def solution(mesh):
    return jax.shard_map(
        shards,
        mesh=mesh,
        in_specs=(P("bank", "feat"), P()),
        out_specs=P("bank", "feat"),
        check_vma=False,
    )
```

```python
import functools

import jax
import jax.numpy as jnp
from jax import lax
from jax.experimental import pallas as pl
from jax.experimental.pallas import tpu as pltpu
from jax.sharding import PartitionSpec as P

TOUCH = 4
BLOCK = 128
SUB = 8
WINDOW = 4
ridge_shift = 0.5


MESH = pl.DeviceIdType.MESH
AHEAD = 3
HOLD = 3
GRAM_AT = (-1, 0, 1, 2, 3, 4)
PASS_AT = (-1, -1, 0, 1, 2, 3)
MOST = 1920


def slot_of(offsets, role, row_start, rows_dev):
    clusters = offsets.shape[0] - 1

    def count(k, found):
        bound = offsets[k]
        first, last = found
        first = first + (bound < row_start).astype(jnp.int32)
        last = last + (bound <= row_start + rows_dev - 1).astype(jnp.int32)
        return first, last

    first, last = lax.fori_loop(1, clusters, count, (jnp.int32(0), jnp.int32(0)))
    middles = last - first - 1
    leading = offsets[first + 1] - row_start
    trailing = row_start + rows_dev - offsets[last]
    early = leading <= trailing
    label = jnp.where(role == 1, first + 1, last - 1)
    label = jnp.where(role == 0, first, jnp.where(role == TOUCH - 1, last, label))
    label = jnp.clip(label, 0, clusters - 1)
    lone = jnp.logical_and(middles == 1, early == (role == 1))
    used = jnp.logical_or(middles == 2, lone)
    used = jnp.logical_or(used, jnp.logical_or(role == 0, role == TOUCH - 1))
    low = jnp.clip(offsets[label] - row_start, 0, rows_dev)
    high = jnp.clip(offsets[label + 1] - row_start, 0, rows_dev)
    return low, jnp.where(used, high, low), label


def own_role():
    feat = lax.axis_index("feat")
    return jnp.where(lax.axis_index("bank") % 2 == 0, feat, TOUCH - 1 - feat)


def neighbours():
    bank, feat = lax.axis_index("bank"), lax.axis_index("feat")
    sibling = feat + 1 - 2 * (feat % 2)
    return bank, sibling, (feat + 2) % TOUCH, (sibling + 2) % TOUCH


def split(value):
    high = value.astype(jnp.bfloat16)
    rest = value - high.astype(jnp.float32)
    middle = rest.astype(jnp.bfloat16)
    low = (rest - middle.astype(jnp.float32)).astype(jnp.bfloat16)
    return high, middle, low


def product(left, right, right_dim):
    first = jnp.concatenate([left[n] for n in (0, 0, 1, 0, 1, 2)], axis=1)
    second = jnp.concatenate([right[n] for n in (0, 1, 0, 2, 1, 0)], axis=right_dim)
    return lax.dot_general(
        first, second, (((1,), (right_dim,)), ((), ())), preferred_element_type=jnp.float32
    )


def split_rows(value):
    high = value.astype(jnp.bfloat16).astype(jnp.float32)
    rest = value - high
    middle = rest.astype(jnp.bfloat16).astype(jnp.float32)
    low = (rest - middle).astype(jnp.bfloat16).astype(jnp.float32)
    return high, middle, low


def factor_block(work):
    panels = BLOCK // SUB
    shape = (SUB, BLOCK)
    lane = lax.broadcasted_iota(jnp.int32, shape, 1)
    sub = lax.broadcasted_iota(jnp.int32, shape, 0)

    def column(tile, c):
        return jnp.broadcast_to(tile[:, c : c + 1], shape)

    def row(tile, i):
        return jnp.broadcast_to(tile[i : i + 1, :], shape)

    tiles = [work[p * SUB : (p + 1) * SUB, :] for p in range(panels)]
    entry_columns = [column(tiles[0], k) for k in range(SUB)]
    for p in range(panels):
        base = p * SUB
        here = jnp.logical_and(lane >= base, lane < base + SUB)
        entry = {(i, k): row(entry_columns[k], i) for i in range(SUB) for k in range(i, SUB)}
        near = range(p + 1, min(p + 1 + WINDOW, panels))
        factors = {r: [column(tiles[r], base + k) for k in range(SUB)] for r in near}
        following = [column(tiles[p + 1], base + SUB + k) for k in range(SUB)] if near else []
        own = jnp.where(here, (lane - base == sub).astype(jnp.float32), tiles[p])
        lines = [row(own, k) for k in range(SUB)]
        for r in near:
            tiles[r] = jnp.where(here, 0.0, tiles[r])
        for k in range(SUB):
            inverse_root = lax.rsqrt(entry[k, k])
            coefficient = {i: entry[k, i] * inverse_root for i in range(k + 1, SUB)}
            for i in range(k + 1, SUB):
                for m in range(i, SUB):
                    entry[i, m] = entry[i, m] - coefficient[i] * coefficient[m]
            lines[k] = lines[k] * inverse_root
            for i in range(k + 1, SUB):
                lines[i] = lines[i] - coefficient[i] * lines[k]
            for r in near:
                scaled = factors[r][k] * inverse_root
                for i in range(k + 1, SUB):
                    factors[r][i] = factors[r][i] - coefficient[i] * scaled
                if r == p + 1:
                    for m in range(SUB):
                        following[m] = following[m] - scaled * row(scaled, m)
                tiles[r] = tiles[r] - scaled * lines[k]
        entry_columns = following
        done = lines[SUB - 1]
        for k in range(SUB - 1):
            done = jnp.where(sub == k, lines[k], done)
        work[base : base + SUB, :] = jnp.where(lane < base + SUB, done, 0.0)
        if p + 1 + WINDOW < panels:
            high, middle, low = split_rows(done)
            left = jnp.concatenate([high, high, middle, high, middle, low], axis=0)
            right = jnp.concatenate([high, middle, high, low, middle, high], axis=0)
            update = lax.dot_general(
                left.astype(jnp.bfloat16),
                right.astype(jnp.bfloat16),
                (((0,), (0,)), ((), ())),
                preferred_element_type=jnp.float32,
            )
            for r in range(p + 1 + WINDOW, panels):
                tiles[r] = jnp.where(here, 0.0, tiles[r]) - update[r * SUB : (r + 1) * SUB, :]


def whitener_kernel(
    bank_count, offsets, own, near_ref, rows_ref, same, opposite, same_mask, opposite_mask, mine, other, planes, inner, final,
    work, near_send, near_receive, keep_sem, show_sem, cross_send, cross_receive, pass_send, pass_receive,
    swap_send, swap_receive, send, receive, local, relay_send,
    relay_receive,
):
    pair_rows, half = own.shape
    rows_dev = 2 * pair_rows
    width = 2 * half
    blocks = width // BLOCK
    strips = half // BLOCK
    skip = (rows_dev - MOST) // 4
    piece = (pair_rows - skip) // 2
    bank, sibling, partner, diagonal = neighbours()
    feat = lax.axis_index("feat")
    side = feat % 2
    parity = feat // 2
    role = own_role()
    meets_left = jnp.logical_and(role == 0, bank > 0)
    meets_right = jnp.logical_and(role == TOUCH - 1, bank < bank_count - 1)
    meets = jnp.logical_or(meets_left, meets_right)
    met = jnp.where(meets_left, bank - 1, bank + 1)
    early = role < 2
    needs = jnp.where(early, 0, skip)
    relays = jnp.where(early, bank < bank_count - 1, bank > 0)
    beyond = jnp.where(early, bank + 1, bank - 1)
    end = jnp.where(feat < 2, TOUCH - 1, 0)
    end_is_partner = jnp.logical_or(feat == 1, feat == 2)

    def remote(source, target, send_sem, receive_sem, device):
        return pltpu.make_async_remote_copy(
            src_ref=source,
            dst_ref=target,
            send_sem=send_sem,
            recv_sem=receive_sem,
            device_id=device,
            device_id_type=MESH,
        )

    def part(base, c):
        return pl.ds(pl.multiple_of(base + c * piece, 16), piece)

    def beside(k, holder):
        return remote(
            own.at[:, pl.ds(k * BLOCK, BLOCK)],
            same.at[holder * strips + k],
            near_send.at[k],
            near_receive.at[k],
            (bank, sibling),
        )

    def keep(k):
        return pltpu.make_async_copy(
            own.at[:, pl.ds(k * BLOCK, BLOCK)], same.at[side * strips + k], keep_sem.at[k]
        )

    def show(k):
        return pltpu.make_async_copy(
            same.at[(1 - side) * strips + k],
            near_ref.at[:, pl.ds(k * BLOCK, BLOCK)],
            show_sem.at[k],
        )

    def crossing(b, base=0):
        return remote(
            same.at[b, part(base, side)],
            opposite.at[b, part(0, side)],
            cross_send.at[b],
            cross_receive.at[b],
            (bank, partner),
        )

    def passing(b):
        return remote(
            opposite.at[b, part(0, side)],
            opposite.at[b, part(0, side)],
            pass_send.at[b],
            pass_receive.at[b],
            (bank, sibling),
        )

    def swap(b):
        span = pl.ds(b * BLOCK, BLOCK), pl.ds(0, (b + 1) * BLOCK)
        return remote(
            mine.at[span], other.at[span], swap_send.at[b], swap_receive.at[b], (met, feat)
        )

    def strip(place, i, device, span, slot=feat):
        columns = pl.ds(span[0], span[1] - span[0])
        return remote(
            final.at[i, columns],
            rows_ref.at[slot, i % strips, columns],
            send.at[place, i % strips],
            receive.at[place, i % strips],
            (bank, device),
        )

    def relay(i, span):
        place = rows_ref.at[end, i % strips, pl.ds(span[0], span[1] - span[0])]
        return remote(
            place, place, relay_send.at[i % strips], relay_receive.at[i % strips], (beyond, feat)
        )

    def spans(i):
        whole = (0, i + 1)
        cut = (i + 2) // 2 if i % 4 != 2 else i // 2
        return whole, (0, cut), (cut, i + 1)

    def stay(i):
        columns = pl.ds(0, i + 1)
        return pltpu.make_async_copy(
            final.at[i, columns], rows_ref.at[feat, i % strips, columns], local.at[i % strips]
        )

    barrier = pltpu.get_barrier_semaphore()
    for k in range(strips):
        keep(k).start()
    for device in (sibling, partner, diagonal):
        pl.semaphore_signal(barrier, inc=1, device_id=(bank, device), device_id_type=MESH)

    @pl.when(meets)
    def _():
        pl.semaphore_signal(barrier, inc=1, device_id=(met, feat), device_id_type=MESH)

    @pl.when(relays)
    def _():
        pl.semaphore_signal(barrier, inc=1, device_id=(beyond, feat), device_id_type=MESH)

    pl.semaphore_wait(barrier, 3 + jnp.where(meets, 1, 0) + jnp.where(relays, 1, 0))

    for k in range(strips):
        beside(k, side).start()

    row_start = bank * rows_dev
    low, high, label = slot_of(offsets, role, row_start, rows_dev)
    count = (offsets[label + 1] - offsets[label]).astype(jnp.float32)
    eye = (
        lax.broadcasted_iota(jnp.int32, (BLOCK, BLOCK), 0)
        == lax.broadcasted_iota(jnp.int32, (BLOCK, BLOCK), 1)
    ).astype(jnp.float32)
    for mask, base, shift in ((same_mask, 0, parity), (opposite_mask, needs, 1 - parity)):
        row = 2 * (base + lax.broadcasted_iota(jnp.int32, mask.shape, 0)) + shift
        inside = jnp.logical_and(row >= low, row < high)
        mask[...] = inside.astype(jnp.bfloat16)

    def cross(b):
        k = b % strips
        owns = side == b // strips

        @pl.when(owns)
        def _():
            keep(k).wait()

        @pl.when(jnp.logical_not(owns))
        def _():
            beside(k, 1 - side).wait_recv()
            show(k).start()

        @pl.when(early)
        def _():
            crossing(b, skip).start()

        @pl.when(jnp.logical_not(early))
        def _():
            crossing(b).start()

    def arrive(b):
        crossing(b).wait_recv()
        passing(b).start()
        if b + AHEAD < blocks:
            cross(b + AHEAD)

    def gram(b):
        passing(b).wait_recv()
        here = pl.ds(b * BLOCK, BLOCK), pl.ds(0, (b + 1) * BLOCK)
        mine[here] = jnp.zeros((BLOCK, (b + 1) * BLOCK), jnp.float32)
        for source, mask in ((same, same_mask), (opposite, opposite_mask)):
            rows = mask.shape[0] // 2

            @pl.loop(0, 2)
            def _(c):
                span = pl.ds(pl.multiple_of(c * rows, rows), rows)
                first = source[b, span] * mask[span]
                second = jnp.concatenate([source[k, span] for k in range(b + 1)], axis=1)
                mine[here] += lax.dot_general(
                    first, second, (((0,), (0,)), ((), ())), preferred_element_type=jnp.float32
                )

        @pl.when(meets)
        def _():
            swap(b).start()

    choices = (jnp.logical_not(meets), meets_right, meets_left)
    end_choices = (
        jnp.logical_not(relays),
        jnp.logical_and(relays, early),
        jnp.logical_and(relays, jnp.logical_not(early)),
    )

    def hand_out(i):
        own_side = 0 if i < strips else 1

        whole = spans(i)[0]
        for choice, span in zip(choices, spans(i)):
            if span[0] < span[1]:

                @pl.when(jnp.logical_and(choice, side == own_side))
                def _():
                    strip(0, i, partner, span).start()

                @pl.when(jnp.logical_and(choice, side != own_side))
                def _():
                    strip(1, i, diagonal, span).start()

        @pl.when(side == own_side)
        def _():
            stay(i).start()

        @pl.when(side != own_side)
        def _():
            strip(2, i, sibling, whole).start()

    for b in range(AHEAD):
        cross(b)
    arrive(0)
    gram(0)
    arrive(1)
    for n in range(3):
        for i in range(blocks - 1):
            planes[n, i * BLOCK : (i + 1) * BLOCK, (i + 1) * BLOCK :] = jnp.zeros(
                (BLOCK, width - (i + 1) * BLOCK), jnp.bfloat16
            )

    def before(i):
        for b in range(blocks):
            if GRAM_AT[b] == i:
                gram(b)
            if PASS_AT[b] == i:
                arrive(b)
        if i == HOLD:
            for k in range(HOLD):
                hand_out(k)

        @pl.when(meets)
        def _():
            swap(i).wait_recv()

        here = pl.ds(i * BLOCK, BLOCK), pl.ds(0, (i + 1) * BLOCK)
        done = i * BLOCK
        total = (mine[here] + jnp.where(meets, other[here], 0.0)) * (1.0 / count)
        square = total[:, done:] + ridge_shift * eye
        if i > 0:
            left = split(total[:, :done])
            groups = [(k, min(k + 2 * BLOCK, done)) for k in range(0, done, 2 * BLOCK)]
            factor = []
            for start, stop in groups:
                inverse = [planes[n, start:stop, :stop] for n in range(3)]
                factor.append(product([value[:, :stop] for value in left], inverse, 1))
            factor = split(jnp.concatenate(factor, axis=1))
            square = square - product(factor, factor, 1)
            for start, stop in groups:
                inverse = [planes[n, start:done, start:stop] for n in range(3)]
                behind = product([value[:, start:] for value in factor], inverse, 0)
                for n, value in enumerate(split(behind)):
                    inner[n, :, start:stop] = value
        work[...] = square

    def after(i):
        done = i * BLOCK
        here = pl.ds(done, BLOCK)
        corner = split(work[...])
        for n in range(3):
            planes[n, here, done : done + BLOCK] = corner[n]
        final[i, i] = corner[0]
        if i > 0:
            behind = [inner[n, :, :done] for n in range(3)]
            for n, value in enumerate(split(-product(corner, behind, 0))):
                planes[n, here, :done] = value
                for k in range(i if n == 0 else 0):
                    final[i, k] = value[:, k * BLOCK : (k + 1) * BLOCK]
        if i >= HOLD:
            hand_out(i)

    @pl.loop(0, blocks)
    def _(j):
        for i in range(blocks):

            @pl.when(j == i)
            def _():
                before(i)

        factor_block(work)
        for i in range(blocks):

            @pl.when(j == i)
            def _():
                after(i)

    for own_side in range(2):
        for i in range(own_side * strips, own_side * strips + strips):
            whole, front, back = spans(i)
            for choice, span, rest in zip(end_choices, (whole, front, back), (None, back, front)):
                for place, is_end in ((0, end_is_partner), (1, jnp.logical_not(end_is_partner))):
                    at_end = jnp.logical_and(side == own_side, is_end)

                    @pl.when(jnp.logical_and(choice, at_end))
                    def _():
                        if span[0] < span[1]:
                            strip(place, i, partner, span, end).wait_recv()
                            if rest is not None:
                                relay(i, span).start()
                        middle = (diagonal, partner)[place]
                        strip(1 - place, i, partner, whole, middle).wait_recv()

        @pl.when(side == own_side)
        def _():
            for i in range(own_side * strips, own_side * strips + strips):
                strip(2, i, sibling, spans(i)[0], sibling).wait_recv()
                stay(i).wait()

    for own_side in range(2):
        for i in range(own_side * strips, own_side * strips + strips):
            whole, front, back = spans(i)
            for choice, span, rest in zip(end_choices[1:], (front, back), (back, front)):

                @pl.when(jnp.logical_and(choice, side == own_side))
                def _():
                    if rest[0] < rest[1]:
                        relay(i, rest).wait_recv()
                    if span[0] < span[1]:
                        relay(i, span).wait_send()

    @pl.when(meets)
    def _():
        for i in range(blocks):
            swap(i).wait_send()

    for b in range(blocks):
        crossing(b).wait_send()
        passing(b).wait_send()
    for k in range(strips):
        beside(k, side).wait_send()
        show(k).wait()
    for i in range(blocks):
        own_side = i // strips
        whole = spans(i)[0]
        for choice, span in zip(choices, spans(i)):
            if span[0] < span[1]:

                @pl.when(jnp.logical_and(choice, side == own_side))
                def _():
                    strip(0, i, partner, span).wait_send()

                @pl.when(jnp.logical_and(choice, side != own_side))
                def _():
                    strip(1, i, diagonal, span).wait_send()

        @pl.when(side != own_side)
        def _():
            strip(2, i, sibling, whole).wait_send()


def whitener_rows(offsets, own):
    pair_rows, half = own.shape
    width = 2 * half
    blocks, strips = width // BLOCK, half // BLOCK
    window = pair_rows - (2 * pair_rows - MOST) // 4
    anywhere = pl.BlockSpec(memory_space=pl.ANY)
    dma = pltpu.SemaphoreType.DMA
    return pl.pallas_call(
        functools.partial(whitener_kernel, lax.axis_size("bank")),
        in_specs=[
            pl.BlockSpec(memory_space=pltpu.SMEM),
            pl.BlockSpec(memory_space=pltpu.HBM),
        ],
        out_specs=[anywhere, anywhere],
        out_shape=[
            jax.ShapeDtypeStruct(own.shape, own.dtype),
            jax.ShapeDtypeStruct((TOUCH, strips, blocks, BLOCK, BLOCK), jnp.bfloat16),
        ],
        scratch_shapes=[
            pltpu.VMEM((blocks, pair_rows, BLOCK), jnp.bfloat16),
            pltpu.VMEM((blocks, window, BLOCK), jnp.bfloat16),
            pltpu.VMEM((pair_rows, BLOCK), jnp.bfloat16),
            pltpu.VMEM((window, BLOCK), jnp.bfloat16),
            pltpu.VMEM((width, width), jnp.float32),
            pltpu.VMEM((width, width), jnp.float32),
            pltpu.VMEM((3, width, width), jnp.bfloat16),
            pltpu.VMEM((3, BLOCK, width), jnp.bfloat16),
            pltpu.VMEM((blocks, blocks, BLOCK, BLOCK), jnp.bfloat16),
            pltpu.VMEM((BLOCK, BLOCK), jnp.float32),
            dma((strips,)),
            dma((strips,)),
            dma((strips,)),
            dma((strips,)),
            dma((blocks,)),
            dma((blocks,)),
            dma((blocks,)),
            dma((blocks,)),
            dma((blocks,)),
            dma((blocks,)),
            dma((3, strips)),
            dma((3, strips)),
            dma((strips,)),
            dma((strips,)),
            dma((strips,)),
        ],
        compiler_params=pltpu.CompilerParams(
            collective_id=0, has_side_effects=True, vmem_limit_bytes=40 << 20
        ),
    )(offsets, own)


def whiten_kernel(offsets, own, near, factor_ref, out_ref, total, bounds):
    step = pl.program_id(0)
    block_pairs, half = own.shape
    strips = half // BLOCK
    rows_dev = pl.num_programs(0) * block_pairs * 2
    bank, feat = lax.axis_index("bank"), lax.axis_index("feat")
    start = step * block_pairs * 2

    @pl.when(step == 0)
    def _():
        for role in range(TOUCH):
            bounds[role], bounds[TOUCH + role], _ = slot_of(
                offsets, jnp.int32(role), bank * rows_dev, rows_dev
            )

    total[...] = jnp.zeros_like(total)
    zero = jnp.zeros((BLOCK, BLOCK), jnp.bfloat16)

    def add(side, low, high, place):
        count = (side + 1) * strips
        row = start + feat // 2 + 2 * lax.broadcasted_iota(jnp.int32, (block_pairs, 1), 0)
        data = own[...] if side == 0 else jnp.concatenate([near[...], own[...]], axis=1)
        keep = jnp.logical_and(row >= low, row < high)
        data = jnp.where(keep, data, jnp.zeros_like(data))
        lines = []
        for i in range(strips):
            last = side * strips + i
            line = [factor_ref[place, i, k] if k <= last else zero for k in range(count)]
            lines.append(jnp.concatenate(line, axis=1))
        total[...] += lax.dot_general(
            data,
            jnp.concatenate(lines, axis=0),
            (((1,), (1,)), ((), ())),
            preferred_element_type=jnp.float32,
        )

    for role in range(TOUCH):
        low, high = bounds[role], bounds[TOUCH + role]
        place = jnp.where(bank % 2 == 0, role, TOUCH - 1 - role)
        inside = jnp.logical_and(start < high, start + 2 * block_pairs > low)
        for side in range(2):

            @pl.when(jnp.logical_and(inside, feat % 2 == side))
            def _():
                add(side, low, high, place)

    out_ref[...] = total[...].astype(jnp.bfloat16)


def whiten(offsets, own, near, factor_rows):
    pair_rows, half = own.shape
    block_pairs = min(256, pair_rows)
    block = pl.BlockSpec((block_pairs, half), lambda i: (i, 0))
    return pl.pallas_call(
        whiten_kernel,
        grid=(pair_rows // block_pairs,),
        in_specs=[
            pl.BlockSpec(memory_space=pltpu.SMEM),
            block,
            block,
            pl.BlockSpec(factor_rows.shape, lambda i: (0, 0, 0, 0, 0)),
        ],
        out_specs=block,
        out_shape=jax.ShapeDtypeStruct((pair_rows, half), jnp.bfloat16),
        scratch_shapes=[
            pltpu.VMEM((block_pairs, half), jnp.float32),
            pltpu.SMEM((2 * TOUCH,), jnp.int32),
        ],
        compiler_params=pltpu.CompilerParams(vmem_limit_bytes=32 << 20),
    )(offsets, own, near, factor_rows)


def shards(bank_rows, offsets):
    near, factor_rows = whitener_rows(offsets, bank_rows)
    return whiten(offsets, bank_rows, near, factor_rows)


def solution(mesh):
    return jax.shard_map(
        shards,
        mesh=mesh,
        in_specs=(P("bank", "feat"), P()),
        out_specs=P("bank", "feat"),
        check_vma=False,
    )
```

```python
import functools

import jax
import jax.numpy as jnp
from jax import lax
from jax.experimental import pallas as pl
from jax.experimental.pallas import tpu as pltpu
from jax.sharding import PartitionSpec as P

TOUCH = 4
BLOCK = 128
SUB = 8
WINDOW = 3
ridge_shift = 0.5


MESH = pl.DeviceIdType.MESH
AHEAD = 3
HOLD = 2
GRAM_AT = (-1, 0, 1, 2, 3, 4)
PASS_AT = (-1, -1, 0, 1, 2, 3)
MOST = 1920


def slot_of(offsets, role, row_start, rows_dev):
    clusters = offsets.shape[0] - 1

    def count(k, found):
        bound = offsets[k]
        first, last = found
        first = first + (bound < row_start).astype(jnp.int32)
        last = last + (bound <= row_start + rows_dev - 1).astype(jnp.int32)
        return first, last

    first, last = lax.fori_loop(1, clusters, count, (jnp.int32(0), jnp.int32(0)))
    middles = last - first - 1
    leading = offsets[first + 1] - row_start
    trailing = row_start + rows_dev - offsets[last]
    early = leading <= trailing
    label = jnp.where(role == 1, first + 1, last - 1)
    label = jnp.where(role == 0, first, jnp.where(role == TOUCH - 1, last, label))
    label = jnp.clip(label, 0, clusters - 1)
    lone = jnp.logical_and(middles == 1, early == (role == 1))
    used = jnp.logical_or(middles == 2, lone)
    used = jnp.logical_or(used, jnp.logical_or(role == 0, role == TOUCH - 1))
    low = jnp.clip(offsets[label] - row_start, 0, rows_dev)
    high = jnp.clip(offsets[label + 1] - row_start, 0, rows_dev)
    return low, jnp.where(used, high, low), label


def own_role():
    feat = lax.axis_index("feat")
    return jnp.where(lax.axis_index("bank") % 2 == 0, feat, TOUCH - 1 - feat)


def neighbours():
    bank, feat = lax.axis_index("bank"), lax.axis_index("feat")
    sibling = feat + 1 - 2 * (feat % 2)
    return bank, sibling, (feat + 2) % TOUCH, (sibling + 2) % TOUCH


def split(value):
    high = value.astype(jnp.bfloat16)
    rest = value - high.astype(jnp.float32)
    middle = rest.astype(jnp.bfloat16)
    low = (rest - middle.astype(jnp.float32)).astype(jnp.bfloat16)
    return high, middle, low


def product(left, right, right_dim):
    first = jnp.concatenate([left[n] for n in (0, 0, 1, 0, 1, 2)], axis=1)
    second = jnp.concatenate([right[n] for n in (0, 1, 0, 2, 1, 0)], axis=right_dim)
    return lax.dot_general(
        first, second, (((1,), (right_dim,)), ((), ())), preferred_element_type=jnp.float32
    )


def split_rows(value):
    high = value.astype(jnp.bfloat16).astype(jnp.float32)
    rest = value - high
    middle = rest.astype(jnp.bfloat16).astype(jnp.float32)
    low = (rest - middle).astype(jnp.bfloat16).astype(jnp.float32)
    return high, middle, low


def factor_block(work):
    panels = BLOCK // SUB
    shape = (SUB, BLOCK)
    lane = lax.broadcasted_iota(jnp.int32, shape, 1)
    sub = lax.broadcasted_iota(jnp.int32, shape, 0)

    def column(tile, c):
        return jnp.broadcast_to(tile[:, c : c + 1], shape)

    def row(tile, i):
        return jnp.broadcast_to(tile[i : i + 1, :], shape)

    tiles = [work[p * SUB : (p + 1) * SUB, :] for p in range(panels)]
    entry_columns = [column(tiles[0], k) for k in range(SUB)]
    for p in range(panels):
        base = p * SUB
        here = jnp.logical_and(lane >= base, lane < base + SUB)
        entry = {(i, k): row(entry_columns[k], i) for i in range(SUB) for k in range(i, SUB)}
        near = range(p + 1, min(p + 1 + WINDOW, panels))
        factors = {r: [column(tiles[r], base + k) for k in range(SUB)] for r in near}
        following = [column(tiles[p + 1], base + SUB + k) for k in range(SUB)] if near else []
        own = jnp.where(here, (lane - base == sub).astype(jnp.float32), tiles[p])
        lines = [row(own, k) for k in range(SUB)]
        for r in near:
            tiles[r] = jnp.where(here, 0.0, tiles[r])
        for k in range(SUB):
            inverse_root = lax.rsqrt(entry[k, k])
            coefficient = {i: entry[k, i] * inverse_root for i in range(k + 1, SUB)}
            for i in range(k + 1, SUB):
                for m in range(i, SUB):
                    entry[i, m] = entry[i, m] - coefficient[i] * coefficient[m]
            lines[k] = lines[k] * inverse_root
            for i in range(k + 1, SUB):
                lines[i] = lines[i] - coefficient[i] * lines[k]
            for r in near:
                scaled = factors[r][k] * inverse_root
                for i in range(k + 1, SUB):
                    factors[r][i] = factors[r][i] - coefficient[i] * scaled
                if r == p + 1:
                    for m in range(SUB):
                        following[m] = following[m] - scaled * row(scaled, m)
                tiles[r] = tiles[r] - scaled * lines[k]
        entry_columns = following
        done = lines[SUB - 1]
        for k in range(SUB - 1):
            done = jnp.where(sub == k, lines[k], done)
        work[base : base + SUB, :] = jnp.where(lane < base + SUB, done, 0.0)
        if p + 1 + WINDOW < panels:
            high, middle, low = split_rows(done)
            left = jnp.concatenate([high, high, middle, high, middle, low], axis=0)
            right = jnp.concatenate([high, middle, high, low, middle, high], axis=0)
            update = lax.dot_general(
                left.astype(jnp.bfloat16),
                right.astype(jnp.bfloat16),
                (((0,), (0,)), ((), ())),
                preferred_element_type=jnp.float32,
            )
            for r in range(p + 1 + WINDOW, panels):
                tiles[r] = jnp.where(here, 0.0, tiles[r]) - update[r * SUB : (r + 1) * SUB, :]


def whitener_kernel(
    bank_count, offsets, own, near_ref, rows_ref, same, opposite, same_mask, opposite_mask, mine, other, planes, inner, final,
    work, near_send, near_receive, keep_sem, show_sem, cross_send, cross_receive, pass_send, pass_receive,
    swap_send, swap_receive, send, receive, local, relay_send,
    relay_receive,
):
    pair_rows, half = own.shape
    rows_dev = 2 * pair_rows
    width = 2 * half
    blocks = width // BLOCK
    strips = half // BLOCK
    skip = (rows_dev - MOST) // 4
    piece = (pair_rows - skip) // 2
    bank, sibling, partner, diagonal = neighbours()
    feat = lax.axis_index("feat")
    side = feat % 2
    parity = feat // 2
    role = own_role()
    meets_left = jnp.logical_and(role == 0, bank > 0)
    meets_right = jnp.logical_and(role == TOUCH - 1, bank < bank_count - 1)
    meets = jnp.logical_or(meets_left, meets_right)
    met = jnp.where(meets_left, bank - 1, bank + 1)
    early = role < 2
    needs = jnp.where(early, 0, skip)
    relays = jnp.where(early, bank < bank_count - 1, bank > 0)
    beyond = jnp.where(early, bank + 1, bank - 1)
    end = jnp.where(feat < 2, TOUCH - 1, 0)
    end_is_partner = jnp.logical_or(feat == 1, feat == 2)

    def remote(source, target, send_sem, receive_sem, device):
        return pltpu.make_async_remote_copy(
            src_ref=source,
            dst_ref=target,
            send_sem=send_sem,
            recv_sem=receive_sem,
            device_id=device,
            device_id_type=MESH,
        )

    def part(base, c):
        return pl.ds(pl.multiple_of(base + c * piece, 16), piece)

    def beside(k, holder):
        return remote(
            own.at[:, pl.ds(k * BLOCK, BLOCK)],
            same.at[holder * strips + k],
            near_send.at[k],
            near_receive.at[k],
            (bank, sibling),
        )

    def keep(k):
        return pltpu.make_async_copy(
            own.at[:, pl.ds(k * BLOCK, BLOCK)], same.at[side * strips + k], keep_sem.at[k]
        )

    def show(k):
        return pltpu.make_async_copy(
            same.at[(1 - side) * strips + k],
            near_ref.at[:, pl.ds(k * BLOCK, BLOCK)],
            show_sem.at[k],
        )

    def crossing(b, base=0):
        return remote(
            same.at[b, part(base, side)],
            opposite.at[b, part(0, side)],
            cross_send.at[b],
            cross_receive.at[b],
            (bank, partner),
        )

    def passing(b):
        return remote(
            opposite.at[b, part(0, side)],
            opposite.at[b, part(0, side)],
            pass_send.at[b],
            pass_receive.at[b],
            (bank, sibling),
        )

    def swap(b):
        span = pl.ds(b * BLOCK, BLOCK), pl.ds(0, (b + 1) * BLOCK)
        return remote(
            mine.at[span], other.at[span], swap_send.at[b], swap_receive.at[b], (met, feat)
        )

    def strip(place, i, device, span, slot=feat):
        columns = pl.ds(span[0], span[1] - span[0])
        return remote(
            final.at[i, columns],
            rows_ref.at[slot, i % strips, columns],
            send.at[place, i % strips],
            receive.at[place, i % strips],
            (bank, device),
        )

    def relay(i, span):
        place = rows_ref.at[end, i % strips, pl.ds(span[0], span[1] - span[0])]
        return remote(
            place, place, relay_send.at[i % strips], relay_receive.at[i % strips], (beyond, feat)
        )

    def spans(i):
        whole = (0, i + 1)
        cut = (i + 2) // 2 if i % 4 != 2 else i // 2
        return whole, (0, cut), (cut, i + 1)

    def stay(i):
        columns = pl.ds(0, i + 1)
        return pltpu.make_async_copy(
            final.at[i, columns], rows_ref.at[feat, i % strips, columns], local.at[i % strips]
        )

    barrier = pltpu.get_barrier_semaphore()
    for k in range(strips):
        keep(k).start()
    for device in (sibling, partner, diagonal):
        pl.semaphore_signal(barrier, inc=1, device_id=(bank, device), device_id_type=MESH)

    @pl.when(meets)
    def _():
        pl.semaphore_signal(barrier, inc=1, device_id=(met, feat), device_id_type=MESH)

    @pl.when(relays)
    def _():
        pl.semaphore_signal(barrier, inc=1, device_id=(beyond, feat), device_id_type=MESH)

    pl.semaphore_wait(barrier, 3 + jnp.where(meets, 1, 0) + jnp.where(relays, 1, 0))

    for k in range(strips):
        beside(k, side).start()

    row_start = bank * rows_dev
    low, high, label = slot_of(offsets, role, row_start, rows_dev)
    count = (offsets[label + 1] - offsets[label]).astype(jnp.float32)
    eye = (
        lax.broadcasted_iota(jnp.int32, (BLOCK, BLOCK), 0)
        == lax.broadcasted_iota(jnp.int32, (BLOCK, BLOCK), 1)
    ).astype(jnp.float32)
    for mask, base, shift in ((same_mask, 0, parity), (opposite_mask, needs, 1 - parity)):
        row = 2 * (base + lax.broadcasted_iota(jnp.int32, mask.shape, 0)) + shift
        inside = jnp.logical_and(row >= low, row < high)
        mask[...] = inside.astype(jnp.bfloat16)

    def cross(b):
        k = b % strips
        owns = side == b // strips

        @pl.when(owns)
        def _():
            keep(k).wait()

        @pl.when(jnp.logical_not(owns))
        def _():
            beside(k, 1 - side).wait_recv()
            show(k).start()

        @pl.when(early)
        def _():
            crossing(b, skip).start()

        @pl.when(jnp.logical_not(early))
        def _():
            crossing(b).start()

    def arrive(b):
        crossing(b).wait_recv()
        passing(b).start()
        if b + AHEAD < blocks:
            cross(b + AHEAD)

    def gram(b):
        passing(b).wait_recv()
        here = pl.ds(b * BLOCK, BLOCK), pl.ds(0, (b + 1) * BLOCK)
        total = jnp.zeros((BLOCK, (b + 1) * BLOCK), jnp.float32)
        for source, mask in ((same, same_mask), (opposite, opposite_mask)):
            first = source[b] * mask[...]
            second = jnp.concatenate([source[k] for k in range(b + 1)], axis=1)
            total = total + lax.dot_general(
                first, second, (((0,), (0,)), ((), ())), preferred_element_type=jnp.float32
            )
        mine[here] = total

        @pl.when(meets)
        def _():
            swap(b).start()

    choices = (jnp.logical_not(meets), meets_right, meets_left)
    end_choices = (
        jnp.logical_not(relays),
        jnp.logical_and(relays, early),
        jnp.logical_and(relays, jnp.logical_not(early)),
    )

    def hand_out(i):
        own_side = 0 if i < strips else 1

        whole = spans(i)[0]
        for choice, span in zip(choices, spans(i)):
            if span[0] < span[1]:

                @pl.when(jnp.logical_and(choice, side == own_side))
                def _():
                    strip(0, i, partner, span).start()

                @pl.when(jnp.logical_and(choice, side != own_side))
                def _():
                    strip(1, i, diagonal, span).start()

        @pl.when(side == own_side)
        def _():
            stay(i).start()

        @pl.when(side != own_side)
        def _():
            strip(2, i, sibling, whole).start()

    for b in range(AHEAD):
        cross(b)
    arrive(0)
    gram(0)
    arrive(1)
    for n in range(3):
        for i in range(blocks - 1):
            planes[n, i * BLOCK : (i + 1) * BLOCK, (i + 1) * BLOCK :] = jnp.zeros(
                (BLOCK, width - (i + 1) * BLOCK), jnp.bfloat16
            )

    def before(i):
        for b in range(blocks):
            if GRAM_AT[b] == i:
                gram(b)
            if PASS_AT[b] == i:
                arrive(b)
        if i == HOLD:
            for k in range(HOLD):
                hand_out(k)

        @pl.when(meets)
        def _():
            swap(i).wait_recv()

        here = pl.ds(i * BLOCK, BLOCK), pl.ds(0, (i + 1) * BLOCK)
        done = i * BLOCK
        total = (mine[here] + jnp.where(meets, other[here], 0.0)) * (1.0 / count)
        square = total[:, done:] + ridge_shift * eye
        if i > 0:
            left = split(total[:, :done])
            groups = [(k, min(k + 2 * BLOCK, done)) for k in range(0, done, 2 * BLOCK)]
            factor = []
            for start, stop in groups:
                inverse = [planes[n, start:stop, :stop] for n in range(3)]
                factor.append(product([value[:, :stop] for value in left], inverse, 1))
            factor = split(jnp.concatenate(factor, axis=1))
            square = square - product(factor, factor, 1)
            for start, stop in groups:
                inverse = [planes[n, start:done, start:stop] for n in range(3)]
                behind = product([value[:, start:] for value in factor], inverse, 0)
                for n, value in enumerate(split(behind)):
                    inner[n, :, start:stop] = value
        work[...] = square

    def after(i):
        done = i * BLOCK
        here = pl.ds(done, BLOCK)
        corner = split(work[...])
        for n in range(3):
            planes[n, here, done : done + BLOCK] = corner[n]
        final[i, i] = corner[0]
        if i > 0:
            behind = [inner[n, :, :done] for n in range(3)]
            for n, value in enumerate(split(-product(corner, behind, 0))):
                planes[n, here, :done] = value
                for k in range(i if n == 0 else 0):
                    final[i, k] = value[:, k * BLOCK : (k + 1) * BLOCK]
        if i >= HOLD:
            hand_out(i)

    @pl.loop(0, blocks)
    def _(j):
        for i in range(blocks):

            @pl.when(j == i)
            def _():
                before(i)

        factor_block(work)
        for i in range(blocks):

            @pl.when(j == i)
            def _():
                after(i)

    for own_side in range(2):
        for i in range(own_side * strips, own_side * strips + strips):
            whole, front, back = spans(i)
            for choice, span, rest in zip(end_choices, (whole, front, back), (None, back, front)):
                for place, is_end in ((0, end_is_partner), (1, jnp.logical_not(end_is_partner))):
                    at_end = jnp.logical_and(side == own_side, is_end)

                    @pl.when(jnp.logical_and(choice, at_end))
                    def _():
                        if span[0] < span[1]:
                            strip(place, i, partner, span, end).wait_recv()
                            if rest is not None:
                                relay(i, span).start()
                        middle = (diagonal, partner)[place]
                        strip(1 - place, i, partner, whole, middle).wait_recv()

        @pl.when(side == own_side)
        def _():
            for i in range(own_side * strips, own_side * strips + strips):
                strip(2, i, sibling, spans(i)[0], sibling).wait_recv()
                stay(i).wait()

    for own_side in range(2):
        for i in range(own_side * strips, own_side * strips + strips):
            whole, front, back = spans(i)
            for choice, span, rest in zip(end_choices[1:], (front, back), (back, front)):

                @pl.when(jnp.logical_and(choice, side == own_side))
                def _():
                    if rest[0] < rest[1]:
                        relay(i, rest).wait_recv()
                    if span[0] < span[1]:
                        relay(i, span).wait_send()

    @pl.when(meets)
    def _():
        for i in range(blocks):
            swap(i).wait_send()

    for b in range(blocks):
        crossing(b).wait_send()
        passing(b).wait_send()
    for k in range(strips):
        beside(k, side).wait_send()
        show(k).wait()
    for i in range(blocks):
        own_side = i // strips
        whole = spans(i)[0]
        for choice, span in zip(choices, spans(i)):
            if span[0] < span[1]:

                @pl.when(jnp.logical_and(choice, side == own_side))
                def _():
                    strip(0, i, partner, span).wait_send()

                @pl.when(jnp.logical_and(choice, side != own_side))
                def _():
                    strip(1, i, diagonal, span).wait_send()

        @pl.when(side != own_side)
        def _():
            strip(2, i, sibling, whole).wait_send()


def whitener_rows(offsets, own):
    pair_rows, half = own.shape
    width = 2 * half
    blocks, strips = width // BLOCK, half // BLOCK
    window = pair_rows - (2 * pair_rows - MOST) // 4
    anywhere = pl.BlockSpec(memory_space=pl.ANY)
    dma = pltpu.SemaphoreType.DMA
    return pl.pallas_call(
        functools.partial(whitener_kernel, lax.axis_size("bank")),
        in_specs=[
            pl.BlockSpec(memory_space=pltpu.SMEM),
            pl.BlockSpec(memory_space=pltpu.HBM),
        ],
        out_specs=[anywhere, anywhere],
        out_shape=[
            jax.ShapeDtypeStruct(own.shape, own.dtype),
            jax.ShapeDtypeStruct((TOUCH, strips, blocks, BLOCK, BLOCK), jnp.bfloat16),
        ],
        scratch_shapes=[
            pltpu.VMEM((blocks, pair_rows, BLOCK), jnp.bfloat16),
            pltpu.VMEM((blocks, window, BLOCK), jnp.bfloat16),
            pltpu.VMEM((pair_rows, BLOCK), jnp.bfloat16),
            pltpu.VMEM((window, BLOCK), jnp.bfloat16),
            pltpu.VMEM((width, width), jnp.float32),
            pltpu.VMEM((width, width), jnp.float32),
            pltpu.VMEM((3, width, width), jnp.bfloat16),
            pltpu.VMEM((3, BLOCK, width), jnp.bfloat16),
            pltpu.VMEM((blocks, blocks, BLOCK, BLOCK), jnp.bfloat16),
            pltpu.VMEM((BLOCK, BLOCK), jnp.float32),
            dma((strips,)),
            dma((strips,)),
            dma((strips,)),
            dma((strips,)),
            dma((blocks,)),
            dma((blocks,)),
            dma((blocks,)),
            dma((blocks,)),
            dma((blocks,)),
            dma((blocks,)),
            dma((3, strips)),
            dma((3, strips)),
            dma((strips,)),
            dma((strips,)),
            dma((strips,)),
        ],
        compiler_params=pltpu.CompilerParams(
            collective_id=0, has_side_effects=True, vmem_limit_bytes=40 << 20
        ),
    )(offsets, own)


def whiten_kernel(offsets, own, near, factor_ref, out_ref, total, bounds):
    step = pl.program_id(0)
    block_pairs, half = own.shape
    strips = half // BLOCK
    rows_dev = pl.num_programs(0) * block_pairs * 2
    bank, feat = lax.axis_index("bank"), lax.axis_index("feat")
    start = step * block_pairs * 2

    @pl.when(step == 0)
    def _():
        for role in range(TOUCH):
            bounds[role], bounds[TOUCH + role], _ = slot_of(
                offsets, jnp.int32(role), bank * rows_dev, rows_dev
            )

    total[...] = jnp.zeros_like(total)
    zero = jnp.zeros((BLOCK, BLOCK), jnp.bfloat16)

    def add(side, low, high, place):
        count = (side + 1) * strips
        row = start + feat // 2 + 2 * lax.broadcasted_iota(jnp.int32, (block_pairs, 1), 0)
        data = own[...] if side == 0 else jnp.concatenate([near[...], own[...]], axis=1)
        keep = jnp.logical_and(row >= low, row < high)
        data = jnp.where(keep, data, jnp.zeros_like(data))
        lines = []
        for i in range(strips):
            last = side * strips + i
            line = [factor_ref[place, i, k] if k <= last else zero for k in range(count)]
            lines.append(jnp.concatenate(line, axis=1))
        total[...] += lax.dot_general(
            data,
            jnp.concatenate(lines, axis=0),
            (((1,), (1,)), ((), ())),
            preferred_element_type=jnp.float32,
        )

    for role in range(TOUCH):
        low, high = bounds[role], bounds[TOUCH + role]
        place = jnp.where(bank % 2 == 0, role, TOUCH - 1 - role)
        inside = jnp.logical_and(start < high, start + 2 * block_pairs > low)
        for side in range(2):

            @pl.when(jnp.logical_and(inside, feat % 2 == side))
            def _():
                add(side, low, high, place)

    out_ref[...] = total[...].astype(jnp.bfloat16)


def whiten(offsets, own, near, factor_rows):
    pair_rows, half = own.shape
    block_pairs = min(256, pair_rows)
    block = pl.BlockSpec((block_pairs, half), lambda i: (i, 0))
    return pl.pallas_call(
        whiten_kernel,
        grid=(pair_rows // block_pairs,),
        in_specs=[
            pl.BlockSpec(memory_space=pltpu.SMEM),
            block,
            block,
            pl.BlockSpec(factor_rows.shape, lambda i: (0, 0, 0, 0, 0)),
        ],
        out_specs=block,
        out_shape=jax.ShapeDtypeStruct((pair_rows, half), jnp.bfloat16),
        scratch_shapes=[
            pltpu.VMEM((block_pairs, half), jnp.float32),
            pltpu.SMEM((2 * TOUCH,), jnp.int32),
        ],
        compiler_params=pltpu.CompilerParams(vmem_limit_bytes=32 << 20),
    )(offsets, own, near, factor_rows)


def shards(bank_rows, offsets):
    near, factor_rows = whitener_rows(offsets, bank_rows)
    return whiten(offsets, bank_rows, near, factor_rows)


def solution(mesh):
    return jax.shard_map(
        shards,
        mesh=mesh,
        in_specs=(P("bank", "feat"), P()),
        out_specs=P("bank", "feat"),
        check_vma=False,
    )
```

```python
import functools

import jax
import jax.numpy as jnp
from jax import lax
from jax.experimental import pallas as pl
from jax.experimental.pallas import tpu as pltpu
from jax.sharding import PartitionSpec as P

TOUCH = 4
BLOCK = 128
SUB = 8
WINDOW = 3
ridge_shift = 0.5


MESH = pl.DeviceIdType.MESH
AHEAD = 4
HOLD = 2
GRAM_AT = (-1, 0, 1, 2, 3, 4)
PASS_AT = (-1, -1, 0, 1, 2, 3)
MOST = 1920


def slot_of(offsets, role, row_start, rows_dev):
    clusters = offsets.shape[0] - 1

    def count(k, found):
        bound = offsets[k]
        first, last = found
        first = first + (bound < row_start).astype(jnp.int32)
        last = last + (bound <= row_start + rows_dev - 1).astype(jnp.int32)
        return first, last

    first, last = lax.fori_loop(1, clusters, count, (jnp.int32(0), jnp.int32(0)))
    middles = last - first - 1
    leading = offsets[first + 1] - row_start
    trailing = row_start + rows_dev - offsets[last]
    early = leading <= trailing
    label = jnp.where(role == 1, first + 1, last - 1)
    label = jnp.where(role == 0, first, jnp.where(role == TOUCH - 1, last, label))
    label = jnp.clip(label, 0, clusters - 1)
    lone = jnp.logical_and(middles == 1, early == (role == 1))
    used = jnp.logical_or(middles == 2, lone)
    used = jnp.logical_or(used, jnp.logical_or(role == 0, role == TOUCH - 1))
    low = jnp.clip(offsets[label] - row_start, 0, rows_dev)
    high = jnp.clip(offsets[label + 1] - row_start, 0, rows_dev)
    return low, jnp.where(used, high, low), label


def own_role():
    feat = lax.axis_index("feat")
    return jnp.where(lax.axis_index("bank") % 2 == 0, feat, TOUCH - 1 - feat)


def neighbours():
    bank, feat = lax.axis_index("bank"), lax.axis_index("feat")
    sibling = feat + 1 - 2 * (feat % 2)
    return bank, sibling, (feat + 2) % TOUCH, (sibling + 2) % TOUCH


def split(value):
    high = value.astype(jnp.bfloat16)
    rest = value - high.astype(jnp.float32)
    middle = rest.astype(jnp.bfloat16)
    low = (rest - middle.astype(jnp.float32)).astype(jnp.bfloat16)
    return high, middle, low


def product(left, right, right_dim):
    first = jnp.concatenate([left[n] for n in (0, 0, 1, 0, 1, 2)], axis=1)
    second = jnp.concatenate([right[n] for n in (0, 1, 0, 2, 1, 0)], axis=right_dim)
    return lax.dot_general(
        first, second, (((1,), (right_dim,)), ((), ())), preferred_element_type=jnp.float32
    )


def split_rows(value):
    high = value.astype(jnp.bfloat16).astype(jnp.float32)
    rest = value - high
    middle = rest.astype(jnp.bfloat16).astype(jnp.float32)
    low = (rest - middle).astype(jnp.bfloat16).astype(jnp.float32)
    return high, middle, low


def factor_block(work):
    panels = BLOCK // SUB
    shape = (SUB, BLOCK)
    lane = lax.broadcasted_iota(jnp.int32, shape, 1)
    sub = lax.broadcasted_iota(jnp.int32, shape, 0)

    def column(tile, c):
        return jnp.broadcast_to(tile[:, c : c + 1], shape)

    def row(tile, i):
        return jnp.broadcast_to(tile[i : i + 1, :], shape)

    tiles = [work[p * SUB : (p + 1) * SUB, :] for p in range(panels)]
    entry_columns = [column(tiles[0], k) for k in range(SUB)]
    for p in range(panels):
        base = p * SUB
        here = jnp.logical_and(lane >= base, lane < base + SUB)
        entry = {(i, k): row(entry_columns[k], i) for i in range(SUB) for k in range(i, SUB)}
        near = range(p + 1, min(p + 1 + WINDOW, panels))
        factors = {r: [column(tiles[r], base + k) for k in range(SUB)] for r in near}
        following = [column(tiles[p + 1], base + SUB + k) for k in range(SUB)] if near else []
        own = jnp.where(here, (lane - base == sub).astype(jnp.float32), tiles[p])
        lines = [row(own, k) for k in range(SUB)]
        for r in near:
            tiles[r] = jnp.where(here, 0.0, tiles[r])
        for k in range(SUB):
            inverse_root = lax.rsqrt(entry[k, k])
            coefficient = {i: entry[k, i] * inverse_root for i in range(k + 1, SUB)}
            for i in range(k + 1, SUB):
                for m in range(i, SUB):
                    entry[i, m] = entry[i, m] - coefficient[i] * coefficient[m]
            lines[k] = lines[k] * inverse_root
            for i in range(k + 1, SUB):
                lines[i] = lines[i] - coefficient[i] * lines[k]
            for r in near:
                scaled = factors[r][k] * inverse_root
                for i in range(k + 1, SUB):
                    factors[r][i] = factors[r][i] - coefficient[i] * scaled
                if r == p + 1:
                    for m in range(SUB):
                        following[m] = following[m] - scaled * row(scaled, m)
                tiles[r] = tiles[r] - scaled * lines[k]
        entry_columns = following
        done = lines[SUB - 1]
        for k in range(SUB - 1):
            done = jnp.where(sub == k, lines[k], done)
        work[base : base + SUB, :] = jnp.where(lane < base + SUB, done, 0.0)
        if p + 1 + WINDOW < panels:
            high, middle, low = split_rows(done)
            left = jnp.concatenate([high, high, middle, high, middle, low], axis=0)
            right = jnp.concatenate([high, middle, high, low, middle, high], axis=0)
            update = lax.dot_general(
                left.astype(jnp.bfloat16),
                right.astype(jnp.bfloat16),
                (((0,), (0,)), ((), ())),
                preferred_element_type=jnp.float32,
            )
            for r in range(p + 1 + WINDOW, panels):
                tiles[r] = jnp.where(here, 0.0, tiles[r]) - update[r * SUB : (r + 1) * SUB, :]


def whitener_kernel(
    bank_count, offsets, own, near_ref, rows_ref, same, opposite, same_mask, opposite_mask, mine, other, planes, inner, final,
    work, near_send, near_receive, keep_sem, show_sem, cross_send, cross_receive, pass_send, pass_receive,
    swap_send, swap_receive, send, receive, local, relay_send,
    relay_receive,
):
    pair_rows, half = own.shape
    rows_dev = 2 * pair_rows
    width = 2 * half
    blocks = width // BLOCK
    strips = half // BLOCK
    skip = (rows_dev - MOST) // 4
    piece = (pair_rows - skip) // 2
    bank, sibling, partner, diagonal = neighbours()
    feat = lax.axis_index("feat")
    side = feat % 2
    parity = feat // 2
    role = own_role()
    meets_left = jnp.logical_and(role == 0, bank > 0)
    meets_right = jnp.logical_and(role == TOUCH - 1, bank < bank_count - 1)
    meets = jnp.logical_or(meets_left, meets_right)
    met = jnp.where(meets_left, bank - 1, bank + 1)
    early = role < 2
    needs = jnp.where(early, 0, skip)
    relays = jnp.where(early, bank < bank_count - 1, bank > 0)
    beyond = jnp.where(early, bank + 1, bank - 1)
    end = jnp.where(feat < 2, TOUCH - 1, 0)
    end_is_partner = jnp.logical_or(feat == 1, feat == 2)

    def remote(source, target, send_sem, receive_sem, device):
        return pltpu.make_async_remote_copy(
            src_ref=source,
            dst_ref=target,
            send_sem=send_sem,
            recv_sem=receive_sem,
            device_id=device,
            device_id_type=MESH,
        )

    def part(base, c):
        return pl.ds(pl.multiple_of(base + c * piece, 16), piece)

    def beside(k, holder):
        return remote(
            own.at[:, pl.ds(k * BLOCK, BLOCK)],
            same.at[holder * strips + k],
            near_send.at[k],
            near_receive.at[k],
            (bank, sibling),
        )

    def keep(k):
        return pltpu.make_async_copy(
            own.at[:, pl.ds(k * BLOCK, BLOCK)], same.at[side * strips + k], keep_sem.at[k]
        )

    def show(k):
        return pltpu.make_async_copy(
            same.at[(1 - side) * strips + k],
            near_ref.at[:, pl.ds(k * BLOCK, BLOCK)],
            show_sem.at[k],
        )

    def crossing(b, base=0):
        return remote(
            same.at[b, part(base, side)],
            opposite.at[b, part(0, side)],
            cross_send.at[b],
            cross_receive.at[b],
            (bank, partner),
        )

    def passing(b):
        return remote(
            opposite.at[b, part(0, side)],
            opposite.at[b, part(0, side)],
            pass_send.at[b],
            pass_receive.at[b],
            (bank, sibling),
        )

    def swap(b):
        span = pl.ds(b * BLOCK, BLOCK), pl.ds(0, (b + 1) * BLOCK)
        return remote(
            mine.at[span], other.at[span], swap_send.at[b], swap_receive.at[b], (met, feat)
        )

    def strip(place, i, device, span, slot=feat):
        columns = pl.ds(span[0], span[1] - span[0])
        return remote(
            final.at[i, columns],
            rows_ref.at[slot, i % strips, columns],
            send.at[place, i % strips],
            receive.at[place, i % strips],
            (bank, device),
        )

    def relay(i, span):
        place = rows_ref.at[end, i % strips, pl.ds(span[0], span[1] - span[0])]
        return remote(
            place, place, relay_send.at[i % strips], relay_receive.at[i % strips], (beyond, feat)
        )

    def spans(i):
        whole = (0, i + 1)
        cut = (i + 2) // 2 if i % 4 != 2 else i // 2
        return whole, (0, cut), (cut, i + 1)

    def stay(i):
        columns = pl.ds(0, i + 1)
        return pltpu.make_async_copy(
            final.at[i, columns], rows_ref.at[feat, i % strips, columns], local.at[i % strips]
        )

    barrier = pltpu.get_barrier_semaphore()
    for k in range(strips):
        keep(k).start()
    for device in (sibling, partner, diagonal):
        pl.semaphore_signal(barrier, inc=1, device_id=(bank, device), device_id_type=MESH)

    @pl.when(meets)
    def _():
        pl.semaphore_signal(barrier, inc=1, device_id=(met, feat), device_id_type=MESH)

    @pl.when(relays)
    def _():
        pl.semaphore_signal(barrier, inc=1, device_id=(beyond, feat), device_id_type=MESH)

    pl.semaphore_wait(barrier, 3 + jnp.where(meets, 1, 0) + jnp.where(relays, 1, 0))

    for k in range(strips):
        beside(k, side).start()

    row_start = bank * rows_dev
    low, high, label = slot_of(offsets, role, row_start, rows_dev)
    count = (offsets[label + 1] - offsets[label]).astype(jnp.float32)
    eye = (
        lax.broadcasted_iota(jnp.int32, (BLOCK, BLOCK), 0)
        == lax.broadcasted_iota(jnp.int32, (BLOCK, BLOCK), 1)
    ).astype(jnp.float32)
    for mask, base, shift in ((same_mask, 0, parity), (opposite_mask, needs, 1 - parity)):
        row = 2 * (base + lax.broadcasted_iota(jnp.int32, mask.shape, 0)) + shift
        inside = jnp.logical_and(row >= low, row < high)
        mask[...] = inside.astype(jnp.bfloat16)

    def cross(b):
        k = b % strips
        owns = side == b // strips

        @pl.when(owns)
        def _():
            keep(k).wait()

        @pl.when(jnp.logical_not(owns))
        def _():
            beside(k, 1 - side).wait_recv()
            show(k).start()

        @pl.when(early)
        def _():
            crossing(b, skip).start()

        @pl.when(jnp.logical_not(early))
        def _():
            crossing(b).start()

    def arrive(b):
        crossing(b).wait_recv()
        passing(b).start()
        if b + AHEAD < blocks:
            cross(b + AHEAD)

    def gram(b):
        passing(b).wait_recv()
        here = pl.ds(b * BLOCK, BLOCK), pl.ds(0, (b + 1) * BLOCK)
        total = jnp.zeros((BLOCK, (b + 1) * BLOCK), jnp.float32)
        for source, mask in ((same, same_mask), (opposite, opposite_mask)):
            first = source[b] * mask[...]
            second = jnp.concatenate([source[k] for k in range(b + 1)], axis=1)
            total = total + lax.dot_general(
                first, second, (((0,), (0,)), ((), ())), preferred_element_type=jnp.float32
            )
        mine[here] = total

        @pl.when(meets)
        def _():
            swap(b).start()

    choices = (jnp.logical_not(meets), meets_right, meets_left)
    end_choices = (
        jnp.logical_not(relays),
        jnp.logical_and(relays, early),
        jnp.logical_and(relays, jnp.logical_not(early)),
    )

    def hand_out(i):
        own_side = 0 if i < strips else 1

        whole = spans(i)[0]
        for choice, span in zip(choices, spans(i)):
            if span[0] < span[1]:

                @pl.when(jnp.logical_and(choice, side == own_side))
                def _():
                    strip(0, i, partner, span).start()

                @pl.when(jnp.logical_and(choice, side != own_side))
                def _():
                    strip(1, i, diagonal, span).start()

        @pl.when(side == own_side)
        def _():
            stay(i).start()

        @pl.when(side != own_side)
        def _():
            strip(2, i, sibling, whole).start()

    for b in range(AHEAD):
        cross(b)
    arrive(0)
    gram(0)
    arrive(1)
    for n in range(3):
        for i in range(blocks - 1):
            planes[n, i * BLOCK : (i + 1) * BLOCK, (i + 1) * BLOCK :] = jnp.zeros(
                (BLOCK, width - (i + 1) * BLOCK), jnp.bfloat16
            )

    def before(i):
        for b in range(blocks):
            if GRAM_AT[b] == i:
                gram(b)
            if PASS_AT[b] == i:
                arrive(b)
        if i == HOLD:
            for k in range(HOLD):
                hand_out(k)

        @pl.when(meets)
        def _():
            swap(i).wait_recv()

        here = pl.ds(i * BLOCK, BLOCK), pl.ds(0, (i + 1) * BLOCK)
        done = i * BLOCK
        total = (mine[here] + jnp.where(meets, other[here], 0.0)) * (1.0 / count)
        square = total[:, done:] + ridge_shift * eye
        if i > 0:
            left = split(total[:, :done])
            groups = [(k, min(k + 2 * BLOCK, done)) for k in range(0, done, 2 * BLOCK)]
            factor = []
            for start, stop in groups:
                inverse = [planes[n, start:stop, :stop] for n in range(3)]
                factor.append(product([value[:, :stop] for value in left], inverse, 1))
            factor = split(jnp.concatenate(factor, axis=1))
            square = square - product(factor, factor, 1)
            for start, stop in groups:
                inverse = [planes[n, start:done, start:stop] for n in range(3)]
                behind = product([value[:, start:] for value in factor], inverse, 0)
                for n, value in enumerate(split(behind)):
                    inner[n, :, start:stop] = value
        work[...] = square

    def after(i):
        done = i * BLOCK
        here = pl.ds(done, BLOCK)
        corner = split(work[...])
        for n in range(3):
            planes[n, here, done : done + BLOCK] = corner[n]
        final[i, i] = corner[0]
        if i > 0:
            behind = [inner[n, :, :done] for n in range(3)]
            for n, value in enumerate(split(-product(corner, behind, 0))):
                planes[n, here, :done] = value
                for k in range(i if n == 0 else 0):
                    final[i, k] = value[:, k * BLOCK : (k + 1) * BLOCK]
        if i >= HOLD:
            hand_out(i)

    @pl.loop(0, blocks)
    def _(j):
        for i in range(blocks):

            @pl.when(j == i)
            def _():
                before(i)

        factor_block(work)
        for i in range(blocks):

            @pl.when(j == i)
            def _():
                after(i)

    for own_side in range(2):
        for i in range(own_side * strips, own_side * strips + strips):
            whole, front, back = spans(i)
            for choice, span, rest in zip(end_choices, (whole, front, back), (None, back, front)):
                for place, is_end in ((0, end_is_partner), (1, jnp.logical_not(end_is_partner))):
                    at_end = jnp.logical_and(side == own_side, is_end)

                    @pl.when(jnp.logical_and(choice, at_end))
                    def _():
                        if span[0] < span[1]:
                            strip(place, i, partner, span, end).wait_recv()
                            if rest is not None:
                                relay(i, span).start()
                        middle = (diagonal, partner)[place]
                        strip(1 - place, i, partner, whole, middle).wait_recv()

        @pl.when(side == own_side)
        def _():
            for i in range(own_side * strips, own_side * strips + strips):
                strip(2, i, sibling, spans(i)[0], sibling).wait_recv()
                stay(i).wait()

    for own_side in range(2):
        for i in range(own_side * strips, own_side * strips + strips):
            whole, front, back = spans(i)
            for choice, span, rest in zip(end_choices[1:], (front, back), (back, front)):

                @pl.when(jnp.logical_and(choice, side == own_side))
                def _():
                    if rest[0] < rest[1]:
                        relay(i, rest).wait_recv()
                    if span[0] < span[1]:
                        relay(i, span).wait_send()

    @pl.when(meets)
    def _():
        for i in range(blocks):
            swap(i).wait_send()

    for b in range(blocks):
        crossing(b).wait_send()
        passing(b).wait_send()
    for k in range(strips):
        beside(k, side).wait_send()
        show(k).wait()
    for i in range(blocks):
        own_side = i // strips
        whole = spans(i)[0]
        for choice, span in zip(choices, spans(i)):
            if span[0] < span[1]:

                @pl.when(jnp.logical_and(choice, side == own_side))
                def _():
                    strip(0, i, partner, span).wait_send()

                @pl.when(jnp.logical_and(choice, side != own_side))
                def _():
                    strip(1, i, diagonal, span).wait_send()

        @pl.when(side != own_side)
        def _():
            strip(2, i, sibling, whole).wait_send()


def whitener_rows(offsets, own):
    pair_rows, half = own.shape
    width = 2 * half
    blocks, strips = width // BLOCK, half // BLOCK
    window = pair_rows - (2 * pair_rows - MOST) // 4
    anywhere = pl.BlockSpec(memory_space=pl.ANY)
    dma = pltpu.SemaphoreType.DMA
    return pl.pallas_call(
        functools.partial(whitener_kernel, lax.axis_size("bank")),
        in_specs=[
            pl.BlockSpec(memory_space=pltpu.SMEM),
            pl.BlockSpec(memory_space=pltpu.HBM),
        ],
        out_specs=[anywhere, anywhere],
        out_shape=[
            jax.ShapeDtypeStruct(own.shape, own.dtype),
            jax.ShapeDtypeStruct((TOUCH, strips, blocks, BLOCK, BLOCK), jnp.bfloat16),
        ],
        scratch_shapes=[
            pltpu.VMEM((blocks, pair_rows, BLOCK), jnp.bfloat16),
            pltpu.VMEM((blocks, window, BLOCK), jnp.bfloat16),
            pltpu.VMEM((pair_rows, BLOCK), jnp.bfloat16),
            pltpu.VMEM((window, BLOCK), jnp.bfloat16),
            pltpu.VMEM((width, width), jnp.float32),
            pltpu.VMEM((width, width), jnp.float32),
            pltpu.VMEM((3, width, width), jnp.bfloat16),
            pltpu.VMEM((3, BLOCK, width), jnp.bfloat16),
            pltpu.VMEM((blocks, blocks, BLOCK, BLOCK), jnp.bfloat16),
            pltpu.VMEM((BLOCK, BLOCK), jnp.float32),
            dma((strips,)),
            dma((strips,)),
            dma((strips,)),
            dma((strips,)),
            dma((blocks,)),
            dma((blocks,)),
            dma((blocks,)),
            dma((blocks,)),
            dma((blocks,)),
            dma((blocks,)),
            dma((3, strips)),
            dma((3, strips)),
            dma((strips,)),
            dma((strips,)),
            dma((strips,)),
        ],
        compiler_params=pltpu.CompilerParams(
            collective_id=0, has_side_effects=True, vmem_limit_bytes=40 << 20
        ),
    )(offsets, own)


def whiten_kernel(offsets, own, near, factor_ref, out_ref, total, bounds):
    step = pl.program_id(0)
    block_pairs, half = own.shape
    strips = half // BLOCK
    rows_dev = pl.num_programs(0) * block_pairs * 2
    bank, feat = lax.axis_index("bank"), lax.axis_index("feat")
    start = step * block_pairs * 2

    @pl.when(step == 0)
    def _():
        for role in range(TOUCH):
            bounds[role], bounds[TOUCH + role], _ = slot_of(
                offsets, jnp.int32(role), bank * rows_dev, rows_dev
            )

    total[...] = jnp.zeros_like(total)
    zero = jnp.zeros((BLOCK, BLOCK), jnp.bfloat16)

    def add(side, low, high, place):
        count = (side + 1) * strips
        row = start + feat // 2 + 2 * lax.broadcasted_iota(jnp.int32, (block_pairs, 1), 0)
        data = own[...] if side == 0 else jnp.concatenate([near[...], own[...]], axis=1)
        keep = jnp.logical_and(row >= low, row < high)
        data = jnp.where(keep, data, jnp.zeros_like(data))
        lines = []
        for i in range(strips):
            last = side * strips + i
            line = [factor_ref[place, i, k] if k <= last else zero for k in range(count)]
            lines.append(jnp.concatenate(line, axis=1))
        total[...] += lax.dot_general(
            data,
            jnp.concatenate(lines, axis=0),
            (((1,), (1,)), ((), ())),
            preferred_element_type=jnp.float32,
        )

    for role in range(TOUCH):
        low, high = bounds[role], bounds[TOUCH + role]
        place = jnp.where(bank % 2 == 0, role, TOUCH - 1 - role)
        inside = jnp.logical_and(start < high, start + 2 * block_pairs > low)
        for side in range(2):

            @pl.when(jnp.logical_and(inside, feat % 2 == side))
            def _():
                add(side, low, high, place)

    out_ref[...] = total[...].astype(jnp.bfloat16)


def whiten(offsets, own, near, factor_rows):
    pair_rows, half = own.shape
    block_pairs = min(512, pair_rows)
    block = pl.BlockSpec((block_pairs, half), lambda i: (i, 0))
    return pl.pallas_call(
        whiten_kernel,
        grid=(pair_rows // block_pairs,),
        in_specs=[
            pl.BlockSpec(memory_space=pltpu.SMEM),
            block,
            block,
            pl.BlockSpec(memory_space=pltpu.VMEM),
        ],
        out_specs=block,
        out_shape=jax.ShapeDtypeStruct((pair_rows, half), jnp.bfloat16),
        scratch_shapes=[
            pltpu.VMEM((block_pairs, half), jnp.float32),
            pltpu.SMEM((2 * TOUCH,), jnp.int32),
        ],
        compiler_params=pltpu.CompilerParams(vmem_limit_bytes=32 << 20),
    )(offsets, own, near, factor_rows)


def shards(bank_rows, offsets):
    near, factor_rows = whitener_rows(offsets, bank_rows)
    return whiten(offsets, bank_rows, near, factor_rows)


def solution(mesh):
    return jax.shard_map(
        shards,
        mesh=mesh,
        in_specs=(P("bank", "feat"), P()),
        out_specs=P("bank", "feat"),
        check_vma=False,
    )
```

```python
import functools

import jax
import jax.numpy as jnp
from jax import lax
from jax.experimental import pallas as pl
from jax.experimental.pallas import tpu as pltpu
from jax.sharding import PartitionSpec as P

TOUCH = 4
BLOCK = 128
SUB = 8
WINDOW = 3
ridge_shift = 0.5


MESH = pl.DeviceIdType.MESH
AHEAD = 4
HOLD = 2
GRAM_AT = (-1, 0, 1, 2, 3, 4)
PASS_AT = (-1, -1, 0, 1, 2, 3)
MOST = 1920


def slot_of(offsets, role, row_start, rows_dev):
    clusters = offsets.shape[0] - 1

    def count(k, found):
        bound = offsets[k]
        first, last = found
        first = first + (bound < row_start).astype(jnp.int32)
        last = last + (bound <= row_start + rows_dev - 1).astype(jnp.int32)
        return first, last

    first, last = lax.fori_loop(1, clusters, count, (jnp.int32(0), jnp.int32(0)))
    middles = last - first - 1
    leading = offsets[first + 1] - row_start
    trailing = row_start + rows_dev - offsets[last]
    early = leading <= trailing
    label = jnp.where(role == 1, first + 1, last - 1)
    label = jnp.where(role == 0, first, jnp.where(role == TOUCH - 1, last, label))
    label = jnp.clip(label, 0, clusters - 1)
    lone = jnp.logical_and(middles == 1, early == (role == 1))
    used = jnp.logical_or(middles == 2, lone)
    used = jnp.logical_or(used, jnp.logical_or(role == 0, role == TOUCH - 1))
    low = jnp.clip(offsets[label] - row_start, 0, rows_dev)
    high = jnp.clip(offsets[label + 1] - row_start, 0, rows_dev)
    return low, jnp.where(used, high, low), label


def own_role():
    feat = lax.axis_index("feat")
    return jnp.where(lax.axis_index("bank") % 2 == 0, feat, TOUCH - 1 - feat)


def neighbours():
    bank, feat = lax.axis_index("bank"), lax.axis_index("feat")
    sibling = feat + 1 - 2 * (feat % 2)
    return bank, sibling, (feat + 2) % TOUCH, (sibling + 2) % TOUCH


def split(value):
    high = value.astype(jnp.bfloat16)
    rest = value - high.astype(jnp.float32)
    middle = rest.astype(jnp.bfloat16)
    low = (rest - middle.astype(jnp.float32)).astype(jnp.bfloat16)
    return high, middle, low


def product(left, right, right_dim):
    first = jnp.concatenate([left[n] for n in (0, 0, 1, 0, 1, 2)], axis=1)
    second = jnp.concatenate([right[n] for n in (0, 1, 0, 2, 1, 0)], axis=right_dim)
    return lax.dot_general(
        first, second, (((1,), (right_dim,)), ((), ())), preferred_element_type=jnp.float32
    )


def split_rows(value):
    high = value.astype(jnp.bfloat16).astype(jnp.float32)
    rest = value - high
    middle = rest.astype(jnp.bfloat16).astype(jnp.float32)
    low = (rest - middle).astype(jnp.bfloat16).astype(jnp.float32)
    return high, middle, low


def factor_block(work):
    panels = BLOCK // SUB
    shape = (SUB, BLOCK)
    lane = lax.broadcasted_iota(jnp.int32, shape, 1)
    sub = lax.broadcasted_iota(jnp.int32, shape, 0)

    def column(tile, c):
        return jnp.broadcast_to(tile[:, c : c + 1], shape)

    def row(tile, i):
        return jnp.broadcast_to(tile[i : i + 1, :], shape)

    tiles = [work[p * SUB : (p + 1) * SUB, :] for p in range(panels)]
    entry_columns = [column(tiles[0], k) for k in range(SUB)]
    for p in range(panels):
        base = p * SUB
        here = jnp.logical_and(lane >= base, lane < base + SUB)
        entry = {(i, k): row(entry_columns[k], i) for i in range(SUB) for k in range(i, SUB)}
        near = range(p + 1, min(p + 1 + WINDOW, panels))
        factors = {r: [column(tiles[r], base + k) for k in range(SUB)] for r in near}
        following = [column(tiles[p + 1], base + SUB + k) for k in range(SUB)] if near else []
        own = jnp.where(here, (lane - base == sub).astype(jnp.float32), tiles[p])
        lines = [row(own, k) for k in range(SUB)]
        for r in near:
            tiles[r] = jnp.where(here, 0.0, tiles[r])
        for k in range(SUB):
            inverse_root = lax.rsqrt(entry[k, k])
            coefficient = {i: entry[k, i] * inverse_root for i in range(k + 1, SUB)}
            for i in range(k + 1, SUB):
                for m in range(i, SUB):
                    entry[i, m] = entry[i, m] - coefficient[i] * coefficient[m]
            lines[k] = lines[k] * inverse_root
            for i in range(k + 1, SUB):
                lines[i] = lines[i] - coefficient[i] * lines[k]
            for r in near:
                scaled = factors[r][k] * inverse_root
                for i in range(k + 1, SUB):
                    factors[r][i] = factors[r][i] - coefficient[i] * scaled
                if r == p + 1:
                    for m in range(SUB):
                        following[m] = following[m] - scaled * row(scaled, m)
                tiles[r] = tiles[r] - scaled * lines[k]
        entry_columns = following
        done = lines[SUB - 1]
        for k in range(SUB - 1):
            done = jnp.where(sub == k, lines[k], done)
        work[base : base + SUB, :] = jnp.where(lane < base + SUB, done, 0.0)
        if p + 1 + WINDOW < panels:
            high, middle, low = split_rows(done)
            left = jnp.concatenate([high, high, middle, high, middle, low], axis=0)
            right = jnp.concatenate([high, middle, high, low, middle, high], axis=0)
            update = lax.dot_general(
                left.astype(jnp.bfloat16),
                right.astype(jnp.bfloat16),
                (((0,), (0,)), ((), ())),
                preferred_element_type=jnp.float32,
            )
            for r in range(p + 1 + WINDOW, panels):
                tiles[r] = jnp.where(here, 0.0, tiles[r]) - update[r * SUB : (r + 1) * SUB, :]


def whitener_kernel(
    bank_count, offsets, own, near_ref, rows_ref, same, opposite, same_mask, opposite_mask, mine, other, planes, inner, final,
    work, near_send, near_receive, keep_sem, show_sem, cross_send, cross_receive, pass_send, pass_receive,
    swap_send, swap_receive, send, receive, local, relay_send,
    relay_receive,
):
    pair_rows, half = own.shape
    rows_dev = 2 * pair_rows
    width = 2 * half
    blocks = width // BLOCK
    strips = half // BLOCK
    skip = (rows_dev - MOST) // 4
    piece = (pair_rows - skip) // 2
    bank, sibling, partner, diagonal = neighbours()
    feat = lax.axis_index("feat")
    side = feat % 2
    parity = feat // 2
    role = own_role()
    meets_left = jnp.logical_and(role == 0, bank > 0)
    meets_right = jnp.logical_and(role == TOUCH - 1, bank < bank_count - 1)
    meets = jnp.logical_or(meets_left, meets_right)
    met = jnp.where(meets_left, bank - 1, bank + 1)
    early = role < 2
    needs = jnp.where(early, 0, skip)
    relays = jnp.where(early, bank < bank_count - 1, bank > 0)
    beyond = jnp.where(early, bank + 1, bank - 1)
    end = jnp.where(feat < 2, TOUCH - 1, 0)
    end_is_partner = jnp.logical_or(feat == 1, feat == 2)

    def remote(source, target, send_sem, receive_sem, device):
        return pltpu.make_async_remote_copy(
            src_ref=source,
            dst_ref=target,
            send_sem=send_sem,
            recv_sem=receive_sem,
            device_id=device,
            device_id_type=MESH,
        )

    def part(base, c):
        return pl.ds(pl.multiple_of(base + c * piece, 16), piece)

    def beside(k, holder):
        return remote(
            own.at[:, pl.ds(k * BLOCK, BLOCK)],
            same.at[holder * strips + k],
            near_send.at[k],
            near_receive.at[k],
            (bank, sibling),
        )

    def keep(k):
        return pltpu.make_async_copy(
            own.at[:, pl.ds(k * BLOCK, BLOCK)], same.at[side * strips + k], keep_sem.at[k]
        )

    def show(k):
        return pltpu.make_async_copy(
            same.at[(1 - side) * strips + k],
            near_ref.at[:, pl.ds(k * BLOCK, BLOCK)],
            show_sem.at[k],
        )

    def crossing(b, base=0):
        return remote(
            same.at[b, part(base, side)],
            opposite.at[b, part(0, side)],
            cross_send.at[b],
            cross_receive.at[b],
            (bank, partner),
        )

    def passing(b):
        return remote(
            opposite.at[b, part(0, side)],
            opposite.at[b, part(0, side)],
            pass_send.at[b],
            pass_receive.at[b],
            (bank, sibling),
        )

    def swap(b):
        span = pl.ds(b * BLOCK, BLOCK), pl.ds(0, (b + 1) * BLOCK)
        return remote(
            mine.at[span], other.at[span], swap_send.at[b], swap_receive.at[b], (met, feat)
        )

    def strip(place, i, device, span, slot=feat):
        columns = pl.ds(span[0], span[1] - span[0])
        return remote(
            final.at[i, columns],
            rows_ref.at[slot, i % strips, columns],
            send.at[place, i % strips],
            receive.at[place, i % strips],
            (bank, device),
        )

    def relay(i, span):
        place = rows_ref.at[end, i % strips, pl.ds(span[0], span[1] - span[0])]
        return remote(
            place, place, relay_send.at[i % strips], relay_receive.at[i % strips], (beyond, feat)
        )

    def spans(i):
        whole = (0, i + 1)
        cut = (i + 2) // 2 if i % 4 != 2 else i // 2
        return whole, (0, cut), (cut, i + 1)

    def stay(i):
        columns = pl.ds(0, i + 1)
        return pltpu.make_async_copy(
            final.at[i, columns], rows_ref.at[feat, i % strips, columns], local.at[i % strips]
        )

    barrier = pltpu.get_barrier_semaphore()
    for k in range(strips):
        keep(k).start()
    for device in (sibling, partner, diagonal):
        pl.semaphore_signal(barrier, inc=1, device_id=(bank, device), device_id_type=MESH)

    @pl.when(meets)
    def _():
        pl.semaphore_signal(barrier, inc=1, device_id=(met, feat), device_id_type=MESH)

    @pl.when(relays)
    def _():
        pl.semaphore_signal(barrier, inc=1, device_id=(beyond, feat), device_id_type=MESH)

    pl.semaphore_wait(barrier, 3 + jnp.where(meets, 1, 0) + jnp.where(relays, 1, 0))

    for k in range(strips):
        beside(k, side).start()

    row_start = bank * rows_dev
    low, high, label = slot_of(offsets, role, row_start, rows_dev)
    count = (offsets[label + 1] - offsets[label]).astype(jnp.float32)
    eye = (
        lax.broadcasted_iota(jnp.int32, (BLOCK, BLOCK), 0)
        == lax.broadcasted_iota(jnp.int32, (BLOCK, BLOCK), 1)
    ).astype(jnp.float32)
    def cross(b):
        k = b % strips
        owns = side == b // strips

        @pl.when(owns)
        def _():
            keep(k).wait()

        @pl.when(jnp.logical_not(owns))
        def _():
            beside(k, 1 - side).wait_recv()
            show(k).start()

        @pl.when(early)
        def _():
            crossing(b, skip).start()

        @pl.when(jnp.logical_not(early))
        def _():
            crossing(b).start()

    def arrive(b):
        crossing(b).wait_recv()
        passing(b).start()
        if b + AHEAD < blocks:
            cross(b + AHEAD)

    def gram(b):
        passing(b).wait_recv()
        here = pl.ds(b * BLOCK, BLOCK), pl.ds(0, (b + 1) * BLOCK)
        total = jnp.zeros((BLOCK, (b + 1) * BLOCK), jnp.float32)
        for source, mask in ((same, same_mask), (opposite, opposite_mask)):
            first = source[b] * mask[...]
            second = jnp.concatenate([source[k] for k in range(b + 1)], axis=1)
            total = total + lax.dot_general(
                first, second, (((0,), (0,)), ((), ())), preferred_element_type=jnp.float32
            )
        mine[here] = total

        @pl.when(meets)
        def _():
            swap(b).start()

    choices = (jnp.logical_not(meets), meets_right, meets_left)
    end_choices = (
        jnp.logical_not(relays),
        jnp.logical_and(relays, early),
        jnp.logical_and(relays, jnp.logical_not(early)),
    )

    def hand_out(i):
        own_side = 0 if i < strips else 1

        whole = spans(i)[0]
        for choice, span in zip(choices, spans(i)):
            if span[0] < span[1]:

                @pl.when(jnp.logical_and(choice, side == own_side))
                def _():
                    strip(0, i, partner, span).start()

                @pl.when(jnp.logical_and(choice, side != own_side))
                def _():
                    strip(1, i, diagonal, span).start()

        @pl.when(side == own_side)
        def _():
            stay(i).start()

        @pl.when(side != own_side)
        def _():
            strip(2, i, sibling, whole).start()

    for b in range(AHEAD):
        cross(b)
    for mask, base, shift in ((same_mask, 0, parity), (opposite_mask, needs, 1 - parity)):
        row = 2 * (base + lax.broadcasted_iota(jnp.int32, mask.shape, 0)) + shift
        inside = jnp.logical_and(row >= low, row < high)
        mask[...] = inside.astype(jnp.bfloat16)

    arrive(0)
    gram(0)
    arrive(1)
    for n in range(3):
        for i in range(blocks - 1):
            planes[n, i * BLOCK : (i + 1) * BLOCK, (i + 1) * BLOCK :] = jnp.zeros(
                (BLOCK, width - (i + 1) * BLOCK), jnp.bfloat16
            )

    def before(i):
        for b in range(blocks):
            if GRAM_AT[b] == i:
                gram(b)
            if PASS_AT[b] == i:
                arrive(b)
        if i == HOLD:
            for k in range(HOLD):
                hand_out(k)

        @pl.when(meets)
        def _():
            swap(i).wait_recv()

        here = pl.ds(i * BLOCK, BLOCK), pl.ds(0, (i + 1) * BLOCK)
        done = i * BLOCK
        total = (mine[here] + jnp.where(meets, other[here], 0.0)) * (1.0 / count)
        square = total[:, done:] + ridge_shift * eye
        if i > 0:
            left = split(total[:, :done])
            groups = [(k, min(k + 2 * BLOCK, done)) for k in range(0, done, 2 * BLOCK)]
            factor = []
            for start, stop in groups:
                inverse = [planes[n, start:stop, :stop] for n in range(3)]
                factor.append(product([value[:, :stop] for value in left], inverse, 1))
            factor = split(jnp.concatenate(factor, axis=1))
            square = square - product(factor, factor, 1)
            for start, stop in groups:
                inverse = [planes[n, start:done, start:stop] for n in range(3)]
                behind = product([value[:, start:] for value in factor], inverse, 0)
                for n, value in enumerate(split(behind)):
                    inner[n, :, start:stop] = value
        work[...] = square

    def after(i):
        done = i * BLOCK
        here = pl.ds(done, BLOCK)
        corner = split(work[...])
        for n in range(3):
            planes[n, here, done : done + BLOCK] = corner[n]
        final[i, i] = corner[0]
        if i > 0:
            behind = [inner[n, :, :done] for n in range(3)]
            for n, value in enumerate(split(-product(corner, behind, 0))):
                planes[n, here, :done] = value
                for k in range(i if n == 0 else 0):
                    final[i, k] = value[:, k * BLOCK : (k + 1) * BLOCK]
        if i >= HOLD:
            hand_out(i)

    @pl.loop(0, blocks)
    def _(j):
        for i in range(blocks):

            @pl.when(j == i)
            def _():
                before(i)

        factor_block(work)
        for i in range(blocks):

            @pl.when(j == i)
            def _():
                after(i)

    for own_side in range(2):
        for i in range(own_side * strips, own_side * strips + strips):
            whole, front, back = spans(i)
            for choice, span, rest in zip(end_choices, (whole, front, back), (None, back, front)):
                for place, is_end in ((0, end_is_partner), (1, jnp.logical_not(end_is_partner))):
                    at_end = jnp.logical_and(side == own_side, is_end)

                    @pl.when(jnp.logical_and(choice, at_end))
                    def _():
                        if span[0] < span[1]:
                            strip(place, i, partner, span, end).wait_recv()
                            if rest is not None:
                                relay(i, span).start()
                        middle = (diagonal, partner)[place]
                        strip(1 - place, i, partner, whole, middle).wait_recv()

        @pl.when(side == own_side)
        def _():
            for i in range(own_side * strips, own_side * strips + strips):
                strip(2, i, sibling, spans(i)[0], sibling).wait_recv()
                stay(i).wait()

    for own_side in range(2):
        for i in range(own_side * strips, own_side * strips + strips):
            whole, front, back = spans(i)
            for choice, span, rest in zip(end_choices[1:], (front, back), (back, front)):

                @pl.when(jnp.logical_and(choice, side == own_side))
                def _():
                    if rest[0] < rest[1]:
                        relay(i, rest).wait_recv()
                    if span[0] < span[1]:
                        relay(i, span).wait_send()

    @pl.when(meets)
    def _():
        for i in range(blocks):
            swap(i).wait_send()

    for b in range(blocks):
        crossing(b).wait_send()
        passing(b).wait_send()
    for k in range(strips):
        beside(k, side).wait_send()
        show(k).wait()
    for i in range(blocks):
        own_side = i // strips
        whole = spans(i)[0]
        for choice, span in zip(choices, spans(i)):
            if span[0] < span[1]:

                @pl.when(jnp.logical_and(choice, side == own_side))
                def _():
                    strip(0, i, partner, span).wait_send()

                @pl.when(jnp.logical_and(choice, side != own_side))
                def _():
                    strip(1, i, diagonal, span).wait_send()

        @pl.when(side != own_side)
        def _():
            strip(2, i, sibling, whole).wait_send()


def whitener_rows(offsets, own):
    pair_rows, half = own.shape
    width = 2 * half
    blocks, strips = width // BLOCK, half // BLOCK
    window = pair_rows - (2 * pair_rows - MOST) // 4
    anywhere = pl.BlockSpec(memory_space=pl.ANY)
    dma = pltpu.SemaphoreType.DMA
    return pl.pallas_call(
        functools.partial(whitener_kernel, lax.axis_size("bank")),
        in_specs=[
            pl.BlockSpec(memory_space=pltpu.SMEM),
            pl.BlockSpec(memory_space=pltpu.HBM),
        ],
        out_specs=[anywhere, anywhere],
        out_shape=[
            jax.ShapeDtypeStruct(own.shape, own.dtype),
            jax.ShapeDtypeStruct((TOUCH, strips, blocks, BLOCK, BLOCK), jnp.bfloat16),
        ],
        scratch_shapes=[
            pltpu.VMEM((blocks, pair_rows, BLOCK), jnp.bfloat16),
            pltpu.VMEM((blocks, window, BLOCK), jnp.bfloat16),
            pltpu.VMEM((pair_rows, BLOCK), jnp.bfloat16),
            pltpu.VMEM((window, BLOCK), jnp.bfloat16),
            pltpu.VMEM((width, width), jnp.float32),
            pltpu.VMEM((width, width), jnp.float32),
            pltpu.VMEM((3, width, width), jnp.bfloat16),
            pltpu.VMEM((3, BLOCK, width), jnp.bfloat16),
            pltpu.VMEM((blocks, blocks, BLOCK, BLOCK), jnp.bfloat16),
            pltpu.VMEM((BLOCK, BLOCK), jnp.float32),
            dma((strips,)),
            dma((strips,)),
            dma((strips,)),
            dma((strips,)),
            dma((blocks,)),
            dma((blocks,)),
            dma((blocks,)),
            dma((blocks,)),
            dma((blocks,)),
            dma((blocks,)),
            dma((3, strips)),
            dma((3, strips)),
            dma((strips,)),
            dma((strips,)),
            dma((strips,)),
        ],
        compiler_params=pltpu.CompilerParams(
            collective_id=0, has_side_effects=True, vmem_limit_bytes=40 << 20
        ),
    )(offsets, own)


def whiten_kernel(offsets, own, near, factor_ref, out_ref, total, bounds):
    step = pl.program_id(0)
    block_pairs, half = own.shape
    strips = half // BLOCK
    rows_dev = pl.num_programs(0) * block_pairs * 2
    bank, feat = lax.axis_index("bank"), lax.axis_index("feat")
    start = step * block_pairs * 2

    @pl.when(step == 0)
    def _():
        for role in range(TOUCH):
            bounds[role], bounds[TOUCH + role], _ = slot_of(
                offsets, jnp.int32(role), bank * rows_dev, rows_dev
            )

    total[...] = jnp.zeros_like(total)
    zero = jnp.zeros((BLOCK, BLOCK), jnp.bfloat16)

    def add(side, low, high, place):
        count = (side + 1) * strips
        row = start + feat // 2 + 2 * lax.broadcasted_iota(jnp.int32, (block_pairs, 1), 0)
        data = own[...] if side == 0 else jnp.concatenate([near[...], own[...]], axis=1)
        keep = jnp.logical_and(row >= low, row < high)
        data = jnp.where(keep, data, jnp.zeros_like(data))
        lines = []
        for i in range(strips):
            last = side * strips + i
            line = [factor_ref[place, i, k] if k <= last else zero for k in range(count)]
            lines.append(jnp.concatenate(line, axis=1))
        total[...] += lax.dot_general(
            data,
            jnp.concatenate(lines, axis=0),
            (((1,), (1,)), ((), ())),
            preferred_element_type=jnp.float32,
        )

    for role in range(TOUCH):
        low, high = bounds[role], bounds[TOUCH + role]
        place = jnp.where(bank % 2 == 0, role, TOUCH - 1 - role)
        inside = jnp.logical_and(start < high, start + 2 * block_pairs > low)
        for side in range(2):

            @pl.when(jnp.logical_and(inside, feat % 2 == side))
            def _():
                add(side, low, high, place)

    out_ref[...] = total[...].astype(jnp.bfloat16)


def whiten(offsets, own, near, factor_rows):
    pair_rows, half = own.shape
    block_pairs = min(512, pair_rows)
    block = pl.BlockSpec((block_pairs, half), lambda i: (i, 0))
    return pl.pallas_call(
        whiten_kernel,
        grid=(pair_rows // block_pairs,),
        in_specs=[
            pl.BlockSpec(memory_space=pltpu.SMEM),
            block,
            block,
            pl.BlockSpec(memory_space=pltpu.VMEM),
        ],
        out_specs=block,
        out_shape=jax.ShapeDtypeStruct((pair_rows, half), jnp.bfloat16),
        scratch_shapes=[
            pltpu.VMEM((block_pairs, half), jnp.float32),
            pltpu.SMEM((2 * TOUCH,), jnp.int32),
        ],
        compiler_params=pltpu.CompilerParams(vmem_limit_bytes=32 << 20),
    )(offsets, own, near, factor_rows)


def shards(bank_rows, offsets):
    near, factor_rows = whitener_rows(offsets, bank_rows)
    return whiten(offsets, bank_rows, near, factor_rows)


def solution(mesh):
    return jax.shard_map(
        shards,
        mesh=mesh,
        in_specs=(P("bank", "feat"), P()),
        out_specs=P("bank", "feat"),
        check_vma=False,
    )
```
